256 devices in a mesh: grp: 2 (over x_hi), row: 8 (over y, core), col: 16 (over z, x_lo).
Axes of the slice: x: 4 (x_hi: 2, x_lo: 2; x = x_hi * 2 + x_lo), y: 4, z: 8, core: 2. Of those that a mesh axis runs over, the one named last changes fastest.
Arguments:
- fields: float32 [2, 8, 6, 128, 2048], P('grp', None, None, 'row', 'col'), may hold values from -6 to 6
- sea_mask: int32 [128, 2048], P('row', 'col'), may hold values 0 or 1
- column_levels: int32 [128, 2048], P('row', 'col'), may hold values from 1 to 8
- w_first: bfloat16 [3, 3, 6, 64], replicated, may hold values from -0.875 to 0.875
- b_first: float32 [64], replicated, may hold values from -3 to 3
- w_second: bfloat16 [3, 3, 64, 64], replicated, may hold values from -0.25 to 0.25
- b_second: float32 [64], replicated, may hold values from -3 to 3
- w_third: bfloat16 [3, 3, 64, 64], replicated, may hold values from -0.25 to 0.25
- b_third: float32 [64], replicated, may hold values from -3 to 3
- w_last: bfloat16 [3, 3, 64, 6], replicated, may hold values from -0.25 to 0.25
- b_last: float32 [6], replicated, may hold values from -3 to 3
Outputs:
- stepped: float32 [2, 8, 6, 128, 2048], P('grp', None, None, 'row', 'col')
The draws below stay inside these ranges and needn't reach their ends.
All inputs are finite; a program needn't handle non-finite values. No bound on the sum of `sea_mask` on one device may be relied on, other than what follows from the above.
Results may differ from the reference program's by a relative error of at most 0.0026.
Values may be sent and summed in bfloat16 or wider, within the bound.
A program may use at most 64 MiB of HBM per device.

```python
import jax
import jax.numpy as jnp
from jax import lax

F = 6
HID = 64
STEPS = 2
L = 8
NLAT = 128
NLON = 2048


def set_ends(values, stream_key, low, high):
    longest = values.shape.index(max(values.shape))
    spots = []
    for shift in (0, 1):
        where = [jax.random.randint(jax.random.fold_in(stream_key, axis), (), 0, length) for axis, length in enumerate(values.shape)]
        where[longest] = (where[longest] + shift) % values.shape[longest]
        spots.append(tuple(where))
    return values.at[spots[0]].set(low).at[spots[1]].set(high)


def steps_of(key, dims, split, smallest, high):
    def one(axis_at, shards_of):
        steps = jax.random.uniform(jax.random.fold_in(jax.random.fold_in(key, 6), axis_at), (shards_of,), jnp.float32, smallest / len(split), high / len(split))
        return jnp.repeat(jnp.exp(steps), dims[axis_at] // shards_of).reshape((-1,) + (1,) * (len(dims) - axis_at - 1))

    factor_of = one(*split[0])
    for cut in split[1:]:
        factor_of = factor_of * one(*cut)
    return factor_of


def gaussian(stream_key, dims, spread, limit, cuts=(), kind=jnp.bfloat16):
    gain = steps_of(stream_key, dims, cuts, -0.22, 0.18) if cuts else 1.0
    array = jax.random.normal(stream_key, dims, jnp.float32) * spread * gain
    return jnp.minimum(jnp.maximum(array, -limit), limit).astype(kind)


def setup_inputs(seed: int = 0) -> dict:
    keys = jax.random.split(jax.random.key(seed), 12)
    fields = gaussian(keys[0], (2, L, F, NLAT, NLON), 1.0, 6.0, ((0, 2), (3, 8), (4, 16)), jnp.float32)
    sea_mask = set_ends((jax.random.randint(keys[1], (NLAT, NLON), 0, 4) < 3).astype(jnp.int32), jax.random.fold_in(keys[1], 1), 0, 1)
    column_levels = set_ends(jax.random.randint(keys[2], (NLAT, NLON), 1, L + 1), jax.random.fold_in(keys[2], 1), 1, L).astype(jnp.int32)
    w_first = gaussian(keys[3], (3, 3, F, HID), (9 * F) ** -0.5, 0.875)
    b_first = gaussian(keys[4], (HID,), 0.5, 3.0, (), jnp.float32)
    w_second = gaussian(keys[5], (3, 3, HID, HID), (9 * HID) ** -0.5, 0.25)
    b_second = gaussian(keys[6], (HID,), 0.5, 3.0, (), jnp.float32)
    w_third = gaussian(keys[7], (3, 3, HID, HID), (9 * HID) ** -0.5, 0.25)
    b_third = gaussian(keys[8], (HID,), 0.5, 3.0, (), jnp.float32)
    w_last = gaussian(keys[9], (3, 3, HID, F), (9 * HID) ** -0.5, 0.25)
    b_last = gaussian(keys[10], (F,), 0.5, 3.0, (), jnp.float32)
    return {"fields": fields, "sea_mask": sea_mask, "column_levels": column_levels, "w_first": w_first, "b_first": b_first, "w_second": w_second, "b_second": b_second, "w_third": w_third, "b_third": b_third, "w_last": w_last, "b_last": b_last}


COURANT = 0.25
FORCE_STEP = 0.5
CORIOLIS = 0.2
ASSELIN = 0.1


def wet_cells(sea_mask, column_levels):
    level_ids = jnp.arange(L, dtype=jnp.int32)[:, None, None]
    return ((level_ids < column_levels[None]) & (sea_mask[None] > 0)).astype(jnp.float32)


def tendency(state, wet_grid):
    masked = state * wet_grid[:, None]
    east_side = jnp.roll(masked, -1, axis=3)
    flux_x = 0.25 * (masked[:, 0:1] + east_side[:, 0:1]) * (masked + east_side)
    div_x = flux_x - jnp.roll(flux_x, 1, axis=3)
    north_side = jnp.concatenate([masked[:, :, 1:], jnp.zeros_like(masked[:, :, :1])], axis=2)
    open_north = (jnp.arange(NLAT, dtype=jnp.int32) < NLAT - 1).astype(jnp.float32)[:, None]
    flux_y = 0.25 * (masked[:, 1:2] + north_side[:, 1:2]) * (masked + north_side) * open_north
    div_y = flux_y - jnp.concatenate([jnp.zeros_like(flux_y[:, :, :1]), flux_y[:, :, :-1]], axis=2)
    sine_lat = jnp.sin(jnp.pi * (jnp.arange(NLAT, dtype=jnp.float32) + 0.5) / NLAT - 0.5 * jnp.pi)[:, None]
    rotation = CORIOLIS * sine_lat * jnp.stack([masked[:, 1], -masked[:, 0]], axis=1)
    return -COURANT * (div_x + div_y) + jnp.concatenate([rotation, jnp.zeros_like(masked[:, 2:])], axis=1)


def conv_layer(source, weight, offset):
    row_count, col_count = source.shape[1], source.shape[2]
    padded = jnp.pad(source, ((0, 0), (1, 1), (0, 0)))
    padded = jnp.concatenate([padded[:, :, -1:], padded, padded[:, :, :1]], axis=2)
    summed = jnp.zeros((weight.shape[3], row_count * col_count), jnp.float32)
    for tap_row in range(3):
        for tap_col in range(3):
            window = padded[:, tap_row:tap_row + row_count, tap_col:tap_col + col_count]
            window = window.reshape(source.shape[0], row_count * col_count).astype(jnp.float32)
            summed = summed + jnp.dot(weight[tap_row, tap_col].astype(jnp.float32).T, window, preferred_element_type=jnp.float32)
    return summed.reshape(weight.shape[3], row_count, col_count) + offset[:, None, None]


def reference(fields, sea_mask, column_levels, w_first, b_first, w_second, b_second, w_third, b_third, w_last, b_last):
    wet_grid = wet_cells(sea_mask, column_levels)
    current = fields[0]
    previous = fields[1]

    def closure_level(level_in):
        hidden = jax.nn.gelu(conv_layer(level_in, w_first, b_first), approximate=True).astype(jnp.bfloat16)
        hidden = jax.nn.gelu(conv_layer(hidden, w_second, b_second), approximate=True).astype(jnp.bfloat16)
        hidden = jax.nn.gelu(conv_layer(hidden, w_third, b_third), approximate=True).astype(jnp.bfloat16)
        return conv_layer(hidden, w_last, b_last).astype(jnp.bfloat16)

    for step_index in range(STEPS):
        advect = tendency(current, wet_grid)
        closure_in = (previous * wet_grid[:, None]).astype(jnp.bfloat16)
        forcing = lax.map(closure_level, closure_in).astype(jnp.float32)
        advanced = wet_grid[:, None] * (previous + advect + FORCE_STEP * forcing)
        filtered = current + ASSELIN * (previous - 2.0 * current + advanced)
        current = advanced
        previous = filtered
    return jnp.stack([current, previous])
```

```python
import functools

import jax
import jax.numpy as jnp
from jax import lax
from jax.experimental import pallas as pl
from jax.experimental.pallas import tpu as pltpu
from jax.sharding import PartitionSpec as P

COURANT = 0.25
FORCE_STEP = 0.5
CORIOLIS = 0.2
ASSELIN = 0.1
F32 = jnp.float32
BF16 = jnp.bfloat16
MESH = pl.DeviceIdType.MESH

F = 6
HID = 64
LANES = 128
ROWS = 16
PAIRS = 72
HALF = 4
RF = ROWS * 8

DIRS = ((1, 0), (-1, 0), (0, 1), (0, -1), (1, 1), (1, -1), (-1, 1), (-1, -1))
OPP = (1, 0, 3, 2, 7, 6, 5, 4)
N_, S_, E_, W_, NE_, NW_, SE_, SW_ = range(8)


def gelu(x):
    inner = 0.7978845608028654 * (x + 0.044715 * (x * x * x))
    return x * (0.5 * (1.0 + jnp.tanh(inner)))


def kernel(
    nrow,
    ncol,
    fields,
    mask_ref,
    levels_ref,
    w1_ref,
    b1_ref,
    w2_ref,
    b2_ref,
    w3_ref,
    b3_ref,
    w4_ref,
    b4_ref,
    out,
    other,
    cur,
    prev,
    depth,
    coriolis,
    stage_n,
    stage_s,
    stage_p,
    halo,
    pack,
    sel,
    wa,
    wb,
    wc,
    wd,
    wtmp,
    wlast,
    bias,
    xb,
    lhs,
    f1e,
    f1o,
    f2e,
    f2o,
    spread,
    zbuf,
    snd,
    tile_ss,
    tile_rs,
    fin_ss,
    fin_rs,
    halo_ss,
    halo_rs,
):
    g = lax.axis_index("grp")
    ri = lax.axis_index("row")
    ci = lax.axis_index("col")
    is0 = g == 0
    partner = {"grp": 1 - g}

    def peer(k):
        dr, dc = DIRS[k]
        where = {}
        if dr:
            where["row"] = lax.rem(ri + dr + nrow, nrow)
        if dc:
            where["col"] = lax.rem(ci + dc + ncol, ncol)
        return where

    barrier = pltpu.get_barrier_semaphore()
    for k in range(8):
        pl.semaphore_signal(barrier, inc=1, device_id=peer(k), device_id_type=MESH)
    pl.semaphore_signal(barrier, inc=1, device_id=partner, device_id_type=MESH)
    pl.semaphore_wait(barrier, 9)

    def tile_copy(l):
        return pltpu.make_async_remote_copy(
            src_ref=fields.at[0, HALF * (1 - g) + l],
            dst_ref=other.at[l],
            send_sem=tile_ss.at[l],
            recv_sem=tile_rs.at[l],
            device_id=partner,
            device_id_type=MESH,
        )

    def final_copy(l):
        return pltpu.make_async_remote_copy(
            src_ref=snd.at[l],
            dst_ref=out.at[0, HALF * g + l],
            send_sem=fin_ss.at[l],
            recv_sem=fin_rs.at[l],
            device_id=partner,
            device_id_type=MESH,
        )

    def halo_copy(t, k):
        if k < 2:
            src = (stage_n if k == N_ else stage_s).at[t]
            dst = halo.at[t, OPP[k]]
        else:
            src = stage_p.at[t]
            dst = pack.at[t, OPP[k] - 2]
        return pltpu.make_async_remote_copy(
            src_ref=src,
            dst_ref=dst,
            send_sem=halo_ss.at[t, k],
            recv_sem=halo_rs.at[t, OPP[k]],
            device_id=peer(k),
            device_id_type=MESH,
        )

    for l in range(HALF):
        tile_copy(l).start()

    lev = jnp.where(mask_ref[...] > 0, levels_ref[...], 0).astype(F32)
    for r in range(ROWS):
        depth[pl.ds(8 * r, 8), :] = jnp.broadcast_to(lev[r : r + 1, :], (8, LANES))
    rows_of = lax.broadcasted_iota(jnp.int32, (RF, LANES), 0)
    lat = (rows_of // 8 + ri * ROWS).astype(F32)
    field_of = rows_of % 8
    sine = CORIOLIS * jnp.sin(jnp.pi * (lat + 0.5) / (nrow * ROWS) - 0.5 * jnp.pi)
    coriolis[...] = jnp.where(field_of == 0, sine, jnp.where(field_of == 1, -sine, 0.0))
    cur[...] = jnp.zeros_like(cur)
    prev[...] = jnp.zeros_like(prev)
    for ref, at in ((f1e, 792), (f1o, 792), (f2e, 720), (f2o, 720)):
        ref[pl.ds(at, 8), :] = jnp.zeros((8, LANES), F32)
    p_of = lax.broadcasted_iota(jnp.int32, (PAIRS, 256), 0)
    j_of = lax.broadcasted_iota(jnp.int32, (PAIRS, 256), 1)
    sel[...] = jnp.where(j_of == lax.rem(2 * p_of + 252, 256), 1.0, 0.0).astype(BF16)

    def tap(ref, a, e):
        if 0 <= a <= 2 and 0 <= e <= 2:
            return ref[a, e].astype(F32)
        return jnp.zeros(ref.shape[2:], F32)

    wtmp[...] = jnp.zeros_like(wtmp)
    for e in range(4):
        for d in range(4):
            for par in range(2):
                wtmp[pl.ds(e * 32 + d * 8, F), pl.ds(par * LANES, LANES)] = jnp.concatenate(
                    [tap(w1_ref, d - par, e), tap(w1_ref, d - par, e - 1)], axis=1
                )
    wa[...] = wtmp[...].astype(BF16)
    for src, dst in ((w2_ref, wb), (w3_ref, wc)):
        for d in range(4):
            for e in range(4):
                for par in range(2):
                    dst[pl.ds(d * 256 + e * 64, HID), pl.ds(par * LANES, LANES)] = jnp.concatenate(
                        [tap(src, d - par, e), tap(src, d - par, e - 1)], axis=1
                    ).astype(BF16)
    wlast[...] = jnp.zeros_like(wlast)
    for a in range(3):
        for e in range(3):
            wlast[a, e, :, pl.ds(0, F)] = w4_ref[a, e].astype(F32)
    for d in range(4):
        for e in range(4):
            for q in range(2):
                wd[pl.ds(d * 256 + e * 64, HID), pl.ds(q * LANES, LANES)] = (
                    tap(wlast, d, e - q) + pltpu.roll(tap(wlast, d - 1, e - q), 8, 1)
                ).astype(BF16)
    bias[...] = jnp.zeros_like(bias)
    for i, b_ref in enumerate((b1_ref, b2_ref, b3_ref)):
        b = b_ref[...]
        bias[pl.ds(i, 1), :] = jnp.concatenate([b, b, b, b], axis=1)
    for at in (0, 8, LANES, LANES + 8):
        bias[pl.ds(3, 1), pl.ds(at, F)] = b4_ref[...]

    lane8 = lax.broadcasted_iota(jnp.int32, (8, LANES), 1)
    south_open = jnp.where(ri > 0, 1.0, 0.0).astype(F32)
    north_open = jnp.where(ri < nrow - 1, 1.0, 0.0).astype(F32)

    def wet_of(l):
        return (HALF * g + l).astype(F32) < depth[...]

    def masked_state(l):
        wet = wet_of(l)
        p = jnp.where(wet, prev[l], 0.0).astype(BF16).astype(F32)
        m = jnp.where(wet, cur[l], 0.0)
        return wet, p, m

    def packed(x):
        total = jnp.zeros((8, LANES), F32)
        for r in range(ROWS):
            part = pltpu.roll(x[8 * r : 8 * r + 8, :], (4 + 8 * r) % LANES, 1)
            total = jnp.where(lane8 // 8 == r, part, total)
        return total

    def send_halos(t, l):
        _, p, m = masked_state(l)
        stage_n[t, pl.ds(0, 32), :] = p[96:128, :]
        stage_n[t, pl.ds(32, 8), :] = m[120:128, :]
        stage_s[t, pl.ds(0, 8), :] = m[0:8, :]
        stage_s[t, pl.ds(8, 32), :] = p[0:32, :]
        stage_p[t, pl.ds(0, 8), :] = packed(p)
        stage_p[t, pl.ds(8, 8), :] = packed(m)
        for k in range(8):
            halo_copy(t, k).start()

    def open_level(l):
        tile_copy(l).wait_recv()
        for f in range(F):
            own = fields[0, HALF * g + l, f]
            oth = other[l, f]
            cur[l, pl.ds(f, ROWS, stride=8), :] = jnp.where(is0, own, oth)
            prev[l, pl.ds(f, ROWS, stride=8), :] = jnp.where(is0, oth, own)
        send_halos(l, l)

    def conv(even, odd, rows, at, weight, i):
        pieces = []
        for d in range(4):
            src = (even, odd)[d % 2]
            off = at + (d // 2) * PAIRS
            pieces.append(src[pl.ds(off, rows), :].astype(BF16))
            pieces.append(src[pl.ds(off + 1, rows), :].astype(BF16))
        x = jnp.concatenate(pieces, axis=1)
        return jnp.dot(x, weight[...], preferred_element_type=F32) + bias[pl.ds(i, 1), :]

    def blank(ref, i):
        ref[pl.ds(i * PAIRS, PAIRS), :] = jnp.zeros((PAIRS, LANES), F32)

    def compute(t, l):
        for k in range(8):
            halo_copy(t, k).wait_recv()
        wet, p, m = masked_state(l)
        first = lane8 % 8 < 4
        low = halo[t, S_]
        high = halo[t, N_]
        mid = jnp.where(first, pack[t, W_ - 2, :, :][0:8], pack[t, E_ - 2, :, :][0:8])
        south = jnp.where(first, pack[t, SW_ - 2, :, :][0:8], pack[t, SE_ - 2, :, :][0:8]) * south_open
        north = jnp.where(first, pack[t, NW_ - 2, :, :][0:8], pack[t, NE_ - 2, :, :][0:8]) * north_open
        main = [low[0:32, :] * south_open, p, high[8:40, :] * north_open]
        side = (
            [pltpu.roll(south, (124 - 8 * (12 + i)) % LANES, 1) for i in range(4)]
            + [pltpu.roll(mid, (124 - 8 * i) % LANES, 1) for i in range(ROWS)]
            + [pltpu.roll(north, (124 - 8 * i) % LANES, 1) for i in range(4)]
        )
        xm = jnp.concatenate(main, axis=0)
        xh = jnp.concatenate(side, axis=0)
        lane = lax.broadcasted_iota(jnp.int32, (192, LANES), 1)
        for e in range(4):
            if e == 0:
                a, b = xm, xh
            else:
                ra = pltpu.roll(xm, LANES - e, 1)
                rb = pltpu.roll(xh, LANES - e, 1)
                keep = lane < LANES - e
                a, b = jnp.where(keep, ra, rb), jnp.where(keep, rb, ra)
            xb[e, :, pl.ds(0, LANES)] = a.astype(BF16)
            xb[e, :, pl.ds(LANES, LANES)] = b.astype(BF16)
        for pair in ((0, 2), (1, 3), (4, 6), (5, 7), (8, 10), (9,)):
            window = jnp.concatenate(
                [xb[e, pl.ds(16 * r, 32), :] for r in pair for e in range(4)], axis=0
            )
            got = lax.dot_general(
                sel[...], window, (((1,), (1,)), ((), ())), preferred_element_type=F32
            )
            for n, r in enumerate(pair):
                lhs[pl.ds(r * PAIRS, PAIRS), :] = got[:, n * LANES : (n + 1) * LANES]
        for at, rows in ((0, 264), (264, 264), (528, 264)):
            y = jnp.dot(
                lhs[pl.ds(at, rows), :].astype(BF16), wa[...], preferred_element_type=F32
            )
            y = gelu(y + bias[pl.ds(0, 1), :])
            f1e[pl.ds(at, rows), :] = y[:, :LANES]
            f1o[pl.ds(at, rows), :] = y[:, LANES:]

        @pl.when(ri == 0)
        def _():
            blank(f1e, 0)
            blank(f1o, 0)
            blank(f1e, 1)

        @pl.when(ri == nrow - 1)
        def _():
            blank(f1o, 9)
            blank(f1e, 10)
            blank(f1o, 10)

        for at, rows in ((0, 360), (360, 360)):
            y = gelu(conv(f1e, f1o, rows, at, wb, 1))
            f2e[pl.ds(at, rows), :] = y[:, :LANES]
            f2o[pl.ds(at, rows), :] = y[:, LANES:]

        @pl.when(ri == 0)
        def _():
            blank(f2e, 0)
            blank(f2o, 0)

        @pl.when(ri == nrow - 1)
        def _():
            blank(f2e, 9)
            blank(f2o, 9)

        for at, rows in ((0, 360), (360, 288)):
            y = gelu(conv(f2e, f2o, rows, at, wc, 2))
            f1e[pl.ds(at, rows), :] = y[:, :LANES]
            f1o[pl.ds(at, rows), :] = y[:, LANES:]

        @pl.when(ri == 0)
        def _():
            blank(f1e, 0)

        @pl.when(ri == nrow - 1)
        def _():
            blank(f1o, 8)

        sums = [jnp.zeros((64, LANES), F32) for _ in range(2)]
        for at, rows in ((0, 288), (288, 288)):
            y = conv(f1e, f1o, rows, at, wd, 3)
            for i in range(rows // PAIRS):
                r = at // PAIRS + i
                for q in range(2):
                    part = y[i * PAIRS : i * PAIRS + 64, q * LANES : (q + 1) * LANES]
                    sums[q] = sums[q] + (pltpu.roll(part, 16 * r, 1) if r else part)
        for q in range(2):
            spread[pl.ds(q, 64, stride=2), :] = sums[q].astype(BF16).astype(F32)
        forcing = spread[...].T

        m3 = m.reshape(ROWS, 8, LANES)
        msouth = low[32:40, :]
        mnorth = high[0:8, :]
        mmid = jnp.where(first, pack[t, W_ - 2, :, :][8:16], pack[t, E_ - 2, :, :][8:16])
        mside = jnp.concatenate(
            [pltpu.roll(mmid, (124 - 8 * i) % LANES, 1) for i in range(ROWS)], axis=0
        )
        lane_rf = lax.broadcasted_iota(jnp.int32, (RF, LANES), 1)
        east = jnp.where(
            lane_rf == LANES - 1, pltpu.roll(mside, LANES - 1, 1), pltpu.roll(m, LANES - 1, 1)
        ).reshape(ROWS, 8, LANES)
        west = jnp.where(lane_rf == 0, pltpu.roll(mside, 1, 1), pltpu.roll(m, 1, 1)).reshape(
            ROWS, 8, LANES
        )
        u = jnp.broadcast_to(m3[:, 0:1, :], m3.shape)
        v = jnp.broadcast_to(m3[:, 1:2, :], m3.shape)
        flux_east = 0.25 * (u + east[:, 0:1, :]) * (m3 + east)
        flux_west = 0.25 * (west[:, 0:1, :] + u) * (west + m3)
        ext = jnp.concatenate([msouth[None], m3, mnorth[None]], axis=0)
        vext = jnp.broadcast_to(ext[:, 1:2, :], ext.shape)
        flux = 0.25 * (vext[:-1] + vext[1:]) * (ext[:-1] + ext[1:])
        flux = jnp.concatenate(
            [flux[0:1] * south_open, flux[1:ROWS], flux[ROWS : ROWS + 1] * north_open], axis=0
        )
        spread_of = flux_east - flux_west + flux[1:] - flux[:-1]
        turn = jnp.where(
            lax.broadcasted_iota(jnp.int32, m3.shape, 1) == 0, v, u
        ) * coriolis[...].reshape(ROWS, 8, LANES)
        advect = (turn - COURANT * spread_of).reshape(RF, LANES)

        pv = prev[l]
        cr = cur[l]
        advanced = jnp.where(wet, pv + advect + FORCE_STEP * forcing, 0.0)
        filtered = cr + ASSELIN * (pv - 2.0 * cr + advanced)
        return advanced, filtered

    open_level(0)

    def body(t, carry):
        step = t // HALF
        l = t - HALF * step

        @pl.when(t < HALF - 1)
        def _():
            open_level(t + 1)

        advanced, filtered = compute(t, l)

        @pl.when(t < HALF)
        def _():
            cur[l] = advanced
            prev[l] = filtered
            send_halos(t + HALF, l)

        @pl.when(t >= HALF)
        def _():
            zbuf[0] = jnp.where(is0, advanced, filtered)
            zbuf[1] = jnp.where(is0, filtered, advanced)
            for f in range(F):
                out[0, HALF * g + l, f] = zbuf[0, pl.ds(f, ROWS, stride=8), :]
                snd[l, f] = zbuf[1, pl.ds(f, ROWS, stride=8), :]
            final_copy(l).start()

        return carry

    lax.fori_loop(0, 2 * HALF, body, 0)

    for l in range(HALF):
        tile_copy(l).wait_send()
        final_copy(l).wait_send()

    def drain(t, carry):
        for k in range(8):
            halo_copy(t, k).wait_send()
        return carry

    lax.fori_loop(0, 2 * HALF, drain, 0)
    for l in range(HALF):
        pltpu.make_async_remote_copy(
            src_ref=snd.at[l],
            dst_ref=out.at[0, HALF * (1 - g) + l],
            send_sem=fin_ss.at[l],
            recv_sem=fin_rs.at[l],
            device_id=partner,
            device_id_type=MESH,
        ).wait_recv()


def solution(mesh):
    nrow = mesh.shape["row"]
    ncol = mesh.shape["col"]

    def shards(fields, sea_mask, column_levels, w1, b1, w2, b2, w3, b3, w4, b4):
        vmem = pl.BlockSpec(memory_space=pltpu.VMEM)
        steps = 2 * HALF
        return pl.pallas_call(
            functools.partial(kernel, nrow, ncol),
            out_shape=jax.ShapeDtypeStruct(fields.shape, F32),
            in_specs=[vmem] * 11,
            out_specs=vmem,
            scratch_shapes=[
                pltpu.VMEM((HALF, F, ROWS, LANES), F32),
                pltpu.VMEM((HALF, RF, LANES), F32),
                pltpu.VMEM((HALF, RF, LANES), F32),
                pltpu.VMEM((RF, LANES), F32),
                pltpu.VMEM((RF, LANES), F32),
                pltpu.VMEM((steps, 40, LANES), F32),
                pltpu.VMEM((steps, 40, LANES), F32),
                pltpu.VMEM((steps, 16, LANES), F32),
                pltpu.VMEM((steps, 2, 40, LANES), F32),
                pltpu.VMEM((steps, 6, 16, LANES), F32),
                pltpu.VMEM((PAIRS, 256), BF16),
                pltpu.VMEM((128, 256), BF16),
                pltpu.VMEM((1024, 256), BF16),
                pltpu.VMEM((1024, 256), BF16),
                pltpu.VMEM((1024, 256), BF16),
                pltpu.VMEM((128, 256), F32),
                pltpu.VMEM((3, 3, HID, LANES), F32),
                pltpu.VMEM((8, 256), F32),
                pltpu.VMEM((4, 192, 256), BF16),
                pltpu.VMEM((792, LANES), F32),
                pltpu.VMEM((800, LANES), F32),
                pltpu.VMEM((800, LANES), F32),
                pltpu.VMEM((728, LANES), F32),
                pltpu.VMEM((728, LANES), F32),
                pltpu.VMEM((RF, LANES), F32),
                pltpu.VMEM((2, RF, LANES), F32),
                pltpu.VMEM((HALF, F, ROWS, LANES), F32),
                pltpu.SemaphoreType.DMA((HALF,)),
                pltpu.SemaphoreType.DMA((HALF,)),
                pltpu.SemaphoreType.DMA((HALF,)),
                pltpu.SemaphoreType.DMA((HALF,)),
                pltpu.SemaphoreType.DMA((steps, 8)),
                pltpu.SemaphoreType.DMA((steps, 8)),
            ],
            compiler_params=pltpu.CompilerParams(
                collective_id=0,
                has_side_effects=True,
                vmem_limit_bytes=48 << 20,
            ),
        )(
            fields,
            sea_mask,
            column_levels,
            w1,
            b1.reshape(1, -1),
            w2,
            b2.reshape(1, -1),
            w3,
            b3.reshape(1, -1),
            w4,
            b4.reshape(1, -1),
        )

    return jax.shard_map(
        shards,
        mesh=mesh,
        in_specs=(P("grp", None, None, "row", "col"), P("row", "col"), P("row", "col")) + (P(),) * 8,
        out_specs=P("grp", None, None, "row", "col"),
        check_vma=False,
    )
```

```python
import functools

import jax
import jax.numpy as jnp
from jax import lax
from jax.experimental import pallas as pl
from jax.experimental.pallas import tpu as pltpu
from jax.sharding import PartitionSpec as P

COURANT = 0.25
FORCE_STEP = 0.5
CORIOLIS = 0.2
ASSELIN = 0.1
F32 = jnp.float32
BF16 = jnp.bfloat16
MESH = pl.DeviceIdType.MESH

F = 6
HID = 64
LANES = 128
ROWS = 16
TILES = 9
WIDE = 16 * TILES
HALF = 4
LV = 2
CHUNKS = HALF // LV
STEPS = 2
RF = ROWS * 8

DIRS = ((1, 0), (-1, 0), (0, 1), (0, -1), (1, 1), (1, -1), (-1, 1), (-1, -1))
OPP = (1, 0, 3, 2, 7, 6, 5, 4)
N_, S_, E_, W_, NE_, NW_, SE_, SW_ = range(8)

BLOCKS = ((0, 0, 4), (0, 4, 2), (0, 6, 3), (0, 9, 2), (1, 0, 3), (1, 3, 2), (1, 5, 3), (1, 8, 2), (2, 0, 2), (2, 2, 2), (2, 4, 3), (2, 7, 2), (3, 0, 4), (3, 4, 3), (3, 7, 2))
LAG = 2

SOUTH = (((0, 0), (0, 1), (1, 0)), ((0, 0), (0, 1)), ((0, 0),))
NORTH = (((9, 1), (10, 0), (10, 1)), ((9, 0), (9, 1)), ((8, 1),))

GELU_TYPE = BF16
K1 = 2.0 * 0.7978845608028654
K2 = 8.0 * 0.7978845608028654 * 0.044715


def gelu_of_half(h):
    inner = h * (h * h * K2 + K1)
    return h * jnp.tanh(inner) + h


def kernel(
    nrow,
    ncol,
    fields,
    mask_hbm,
    levels_hbm,
    w1_hbm,
    b1_hbm,
    w2_hbm,
    b2_hbm,
    w3_hbm,
    b3_hbm,
    w4_hbm,
    b4_hbm,
    out,
    mine,
    mask_ref,
    levels_ref,
    w1_ref,
    b1_ref,
    w2_ref,
    b2_ref,
    w3_ref,
    b3_ref,
    w4_ref,
    b4_ref,
    other,
    cur,
    prev,
    depth,
    coriolis,
    stage_n,
    stage_s,
    stage_p,
    halo,
    pack_side,
    pack_diag,
    sel,
    wa,
    wb,
    wc,
    wd,
    wtmp,
    wlast,
    bias,
    xb,
    lhs,
    f1e,
    f1o,
    f2e,
    f2o,
    f3e,
    f3o,
    spread,
    moved,
    zbuf,
    snd,
    load_s,
    tile_ss,
    tile_rs,
    fin_ss,
    fin_rs,
    halo_ss,
    halo_rs,
):
    g = lax.axis_index("grp")
    ri = lax.axis_index("row")
    ci = lax.axis_index("col")
    is0 = g == 0
    partner = {"grp": 1 - g}

    def peer(k):
        dr, dc = DIRS[k]
        where = {}
        if dr:
            where["row"] = lax.rem(ri + dr + nrow, nrow)
        if dc:
            where["col"] = lax.rem(ci + dc + ncol, ncol)
        return where

    barrier = pltpu.get_barrier_semaphore()
    for k in range(8):
        pl.semaphore_signal(barrier, inc=1, device_id=peer(k), device_id_type=MESH)
    pl.semaphore_signal(barrier, inc=1, device_id=partner, device_id_type=MESH)

    loads = [
        pltpu.make_async_copy(src, dst, load_s.at[i])
        for i, (src, dst) in enumerate(
            (
                (mask_hbm, mask_ref),
                (levels_hbm, levels_ref),
                (w1_hbm, w1_ref),
                (b1_hbm, b1_ref),
                (b2_hbm, b2_ref),
                (b3_hbm, b3_ref),
                (b4_hbm, b4_ref),
                (w2_hbm, w2_ref),
                (w3_hbm, w3_ref),
                (w4_hbm, w4_ref),
                (fields.at[0, pl.ds(HALF * g, HALF)], mine),
            )
        )
    ]
    for load in loads:
        load.start()

    pl.semaphore_wait(barrier, 9)

    def tile_copy(c):
        return pltpu.make_async_remote_copy(
            src_ref=fields.at[0, pl.ds(HALF * (1 - g) + LV * c, LV)],
            dst_ref=other.at[pl.ds(LV * c, LV)],
            send_sem=tile_ss.at[c],
            recv_sem=tile_rs.at[c],
            device_id=partner,
            device_id_type=MESH,
        )

    def final_copy(c, owner):
        return pltpu.make_async_remote_copy(
            src_ref=snd.at[pl.ds(LV * c, LV)],
            dst_ref=out.at[0, pl.ds(HALF * owner + LV * c, LV)],
            send_sem=fin_ss.at[c],
            recv_sem=fin_rs.at[c],
            device_id=partner,
            device_id_type=MESH,
        )

    def halo_copy(t, k):
        if k < 2:
            src = (stage_n if k == N_ else stage_s).at[t]
            dst = halo.at[t, OPP[k]]
        elif k < 4:
            src = stage_p.at[t]
            dst = pack_side.at[t, OPP[k] - 2]
        else:
            src = stage_p.at[t, pl.ds(0, 8 * LV)]
            dst = pack_diag.at[t, OPP[k] - 4]
        return pltpu.make_async_remote_copy(
            src_ref=src,
            dst_ref=dst,
            send_sem=halo_ss.at[t, k],
            recv_sem=halo_rs.at[t, OPP[k]],
            device_id=peer(k),
            device_id_type=MESH,
        )

    for c in range(CHUNKS):
        tile_copy(c).start()
    for load in loads:
        load.wait()

    lev = jnp.where(mask_ref[...] > 0, levels_ref[...], 0).astype(F32)
    for r in range(ROWS):
        depth[pl.ds(8 * r, 8), :] = jnp.broadcast_to(lev[r : r + 1, :], (8, LANES))
    rows_of = lax.broadcasted_iota(jnp.int32, (RF, LANES), 0)
    lat = (rows_of // 8 + ri * ROWS).astype(F32)
    field_of = rows_of % 8
    sine = CORIOLIS * jnp.sin(jnp.pi * (lat + 0.5) / (nrow * ROWS) - 0.5 * jnp.pi)
    coriolis[...] = jnp.where(field_of == 0, sine, jnp.where(field_of == 1, -sine, 0.0))
    cur[...] = jnp.zeros_like(cur)
    prev[...] = jnp.zeros_like(prev)
    m_of = lax.broadcasted_iota(jnp.int32, (8 * TILES, 256), 0)
    j_of = lax.broadcasted_iota(jnp.int32, (8 * TILES, 256), 1)
    pair_of = TILES * (m_of % 8) + m_of // 8
    sel[...] = jnp.where(j_of == (2 * pair_of + 252) % 256, 1.0, 0.0).astype(BF16)

    lane8 = lax.broadcasted_iota(jnp.int32, (8, LANES), 1)
    south_open = jnp.where(ri > 0, 1.0, 0.0).astype(F32)
    north_open = jnp.where(ri < nrow - 1, 1.0, 0.0).astype(F32)

    def masked_state(l):
        wet = (HALF * g + l).astype(F32) < depth[...]
        p = jnp.where(wet, prev[l], 0.0).astype(BF16).astype(F32)
        m = jnp.where(wet, cur[l], 0.0)
        return wet, p, m

    def packed(x):
        total = jnp.zeros((8, LANES), F32)
        for r in range(ROWS):
            part = pltpu.roll(x[8 * r : 8 * r + 8, :], (4 + 8 * r) % LANES, 1)
            total = jnp.where(lane8 // 8 == r, part, total)
        return total

    def halves(x):
        high = x.astype(BF16).astype(F32)
        return high, x - high

    def send_halos(t, c):
        rows = [[], [], []]
        for i in range(LV):
            _, p, m = masked_state(LV * c + i)
            stage_n[t, i, pl.ds(0, 32), :] = p[96:128, :].astype(BF16)
            stage_n[t, i, pl.ds(32, 16), :] = jnp.concatenate(
                halves(m[120:128, :]), axis=0
            ).astype(BF16)
            stage_s[t, i, pl.ds(0, 32), :] = p[0:32, :].astype(BF16)
            stage_s[t, i, pl.ds(32, 16), :] = jnp.concatenate(halves(m[0:8, :]), axis=0).astype(
                BF16
            )
            rows[0].append(packed(p))
            high, low = halves(packed(m))
            rows[1].append(high)
            rows[2].append(low)
        for j in range(3):
            stage_p[t, pl.ds(8 * LV * j, 8 * LV), :] = jnp.concatenate(rows[j], axis=0).astype(BF16)
        for k in range(8):
            halo_copy(t, k).start()

    def side(t, k, i, j):
        if k < 4:
            part = pack_side[t, k - 2, pl.ds(8 * LV * j, 8 * LV), :]
        else:
            part = pack_diag[t, k - 4]
        return part.astype(F32)[8 * i : 8 * i + 8, :]

    def edge_row(t, k, i):
        part = halo[t, k, i, pl.ds(32, 16), :].astype(F32)
        return part[0:8, :] + part[8:16, :]

    def open_chunk(c):
        tile_copy(c).wait_recv()
        for i in range(LV):
            l = LV * c + i
            for f in range(F):
                own = mine[l, f]
                oth = other[l, f]
                cur[l, pl.ds(f, ROWS, stride=8), :] = jnp.where(is0, own, oth)
                prev[l, pl.ds(f, ROWS, stride=8), :] = jnp.where(is0, oth, own)
        send_halos(c, c)

    def fill_lhs(t, both):
        for i in range(LV):
            p = both[i][1]
            first = lane8 % 8 < 4
            mid, south, north = [
                jnp.where(first, side(t, w, i, 0), side(t, e, i, 0))
                for w, e in ((W_, E_), (SW_, SE_), (NW_, NE_))
            ]
            south = south * south_open
            north = north * north_open
            low = halo[t, S_, i, pl.ds(0, 32), :].astype(F32)
            high = halo[t, N_, i, pl.ds(0, 32), :].astype(F32)
            xm = jnp.concatenate([low * south_open, p, high * north_open], axis=0)
            xh = jnp.concatenate(
                [pltpu.roll(south, (124 - 8 * (12 + j)) % LANES, 1) for j in range(4)]
                + [pltpu.roll(mid, (124 - 8 * j) % LANES, 1) for j in range(ROWS)]
                + [pltpu.roll(north, (124 - 8 * j) % LANES, 1) for j in range(4)],
                axis=0,
            )
            lane = lax.broadcasted_iota(jnp.int32, (192, LANES), 1)
            for e in range(4):
                if e == 0:
                    a, b = xm, xh
                else:
                    ra = pltpu.roll(xm, LANES - e, 1)
                    rb = pltpu.roll(xh, LANES - e, 1)
                    keep = lane < LANES - e
                    a, b = jnp.where(keep, ra, rb), jnp.where(keep, rb, ra)
                xb[i, e, :, pl.ds(0, LANES)] = a.astype(BF16)
                xb[i, e, :, pl.ds(LANES, LANES)] = b.astype(BF16)
        for group in ((0, 2), (1, 3), (4, 6), (5, 7), (8, 10), (9,)):
            got = []
            for i in range(LV):
                window = jnp.concatenate(
                    [xb[i, e, pl.ds(16 * r, 32), :] for r in group for e in range(4)], axis=0
                )
                got.append(
                    lax.dot_general(
                        sel[...], window, (((1,), (1,)), ((), ())), preferred_element_type=F32
                    ).reshape(TILES, 1, 8, LANES * len(group))
                )
            merged = jnp.concatenate(got, axis=1).reshape(WIDE, LANES * len(group)).astype(BF16)
            for n, r in enumerate(group):
                lhs[r] = merged[:, n * LANES : (n + 1) * LANES]

    stores = ((f1e, f1o), (f2e, f2o), (f3e, f3o))
    weights = (wa, wb, wc, wd)

    def block_dot(layer, r0, n):
        if layer == 0:
            x = lhs[pl.ds(r0, n)].reshape(n * WIDE, LANES)
        elif layer == 3:
            x = jnp.concatenate(
                [
                    src[pl.ds(r0, n), pl.ds(16 * shift, WIDE), :].reshape(n * WIDE, LANES)
                    for src in stores[2]
                    for shift in range(2)
                ],
                axis=1,
            )
        else:
            pieces = []
            for d in range(4):
                src = stores[layer - 1][d % 2]
                for shift in range(2):
                    pieces.append(
                        src[pl.ds(r0 + d // 2, n), pl.ds(16 * shift, WIDE), :].reshape(
                            n * WIDE, LANES
                        )
                    )
            x = jnp.concatenate(pieces, axis=1)
        return jnp.dot(x, weights[layer][...], preferred_element_type=F32)

    def block_store(layer, r0, n, y, sums):
        if layer == 3:
            lanes = lax.broadcasted_iota(jnp.int32, (WIDE, LANES), 1)
            for i in range(n):
                r = r0 + i
                for q in range(2):
                    part = y[i * WIDE : (i + 1) * WIDE, q * LANES : (q + 1) * LANES]
                    if r == 0:
                        part = jnp.where(lanes >= 16, part, 0.0)
                    if r == ROWS // 2:
                        part = jnp.where(lanes < 16, part, 0.0)
                    if r != 1:
                        part = pltpu.roll(part, (16 * (r - 1)) % LANES, 1)
                    sums[q] = part if sums[q] is None else sums[q] + part
            return
        y = y + bias[pl.ds(layer, 1), :]
        h = gelu_of_half(y.astype(GELU_TYPE))
        for par in range(2):
            dst = stores[layer][par]
            for i in range(n):
                piece = h[i * WIDE : (i + 1) * WIDE, par * LANES : (par + 1) * LANES]
                if (r0 + i, par) in SOUTH[layer]:
                    piece = piece * south_open.astype(GELU_TYPE)
                if (r0 + i, par) in NORTH[layer]:
                    piece = piece * north_open.astype(GELU_TYPE)
                dst[r0 + i, pl.ds(0, WIDE), :] = piece.astype(BF16)
                edge = piece[0:16, :].astype(F32)
                edge = jnp.concatenate(
                    [pltpu.roll(edge[0:8], 7, 0), pltpu.roll(edge[8:16], 7, 0)], axis=0
                )
                dst[r0 + i, pl.ds(WIDE, 16), :] = edge.astype(BF16)

    def tendency(t, i, m):
        first = lane8 % 8 < 4
        m3 = m.reshape(ROWS, 8, LANES)
        msouth = edge_row(t, S_, i)
        mnorth = edge_row(t, N_, i)
        mmid = jnp.where(
            first,
            side(t, W_, i, 1) + side(t, W_, i, 2),
            side(t, E_, i, 1) + side(t, E_, i, 2),
        )
        mside = jnp.concatenate(
            [pltpu.roll(mmid, (124 - 8 * j) % LANES, 1) for j in range(ROWS)], axis=0
        )
        lane_rf = lax.broadcasted_iota(jnp.int32, (RF, LANES), 1)
        east = jnp.where(
            lane_rf == LANES - 1, pltpu.roll(mside, LANES - 1, 1), pltpu.roll(m, LANES - 1, 1)
        ).reshape(ROWS, 8, LANES)
        west = jnp.where(lane_rf == 0, pltpu.roll(mside, 1, 1), pltpu.roll(m, 1, 1)).reshape(
            ROWS, 8, LANES
        )
        u = jnp.broadcast_to(m3[:, 0:1, :], m3.shape)
        v = jnp.broadcast_to(m3[:, 1:2, :], m3.shape)
        flux_east = (u + east[:, 0:1, :]) * (m3 + east)
        flux_west = (west[:, 0:1, :] + u) * (west + m3)
        ext = jnp.concatenate([msouth[None], m3, mnorth[None]], axis=0)
        vext = jnp.broadcast_to(ext[:, 1:2, :], ext.shape)
        flux = (vext[:-1] + vext[1:]) * (ext[:-1] + ext[1:])
        flux = jnp.concatenate(
            [flux[0:1] * south_open, flux[1:ROWS], flux[ROWS : ROWS + 1] * north_open], axis=0
        )
        spread_of = flux_east - flux_west + flux[1:] - flux[:-1]
        turn = jnp.where(
            lax.broadcasted_iota(jnp.int32, m3.shape, 1) == 0, v, u
        ) * coriolis[...].reshape(ROWS, 8, LANES)
        return (turn - (0.25 * COURANT) * spread_of).reshape(RF, LANES)

    def compute(t, c):
        for k in range(8):
            halo_copy(t, k).wait_recv()
        both = [masked_state(LV * c + i) for i in range(LV)]
        fill_lhs(t, both)
        sums = [None, None]
        waiting = []
        for n, block in enumerate(BLOCKS):
            y = block_dot(*block)
            waiting.append((*block, y))
            if len(waiting) > LAG:
                block_store(*waiting.pop(0), sums)
            if n in (5, 9):
                i = (5, 9).index(n)
                moved[i] = prev[LV * c + i] + tendency(t, i, both[i][2])
        for item in waiting:
            block_store(*item, sums)
        for q in range(2):
            total = (sums[q] + bias[pl.ds(3, 1), pl.ds(0, LANES)]).astype(BF16).astype(F32)
            for p in range(TILES):
                for i in range(LV):
                    at = 16 * p + 8 * i
                    spread[i, pl.ds(2 * p + q, 8, stride=2 * TILES), :] = total[at : at + 8, :]
        done = []
        for i in range(LV):
            wet = both[i][0]
            forcing = spread[i, pl.ds(0, LANES), :].T
            pv = prev[LV * c + i]
            cr = cur[LV * c + i]
            advanced = jnp.where(wet, moved[i] + FORCE_STEP * forcing, 0.0)
            filtered = cr + ASSELIN * (pv - 2.0 * cr + advanced)
            done.append((advanced, filtered))
        return done

    open_chunk(0)

    def tap(ref, a, e):
        if 0 <= a <= 2 and 0 <= e <= 2:
            return ref[a, e].astype(F32)
        return jnp.zeros(ref.shape[2:], F32)

    wtmp[...] = jnp.zeros_like(wtmp)
    for e in range(4):
        for d in range(4):
            for par in range(2):
                wtmp[pl.ds(e * 32 + d * 8, F), pl.ds(par * LANES, LANES)] = 0.5 * jnp.concatenate(
                    [tap(w1_ref, d - par, e), tap(w1_ref, d - par, e - 1)], axis=1
                )
    wa[...] = wtmp[...].astype(BF16)
    for src, dst in ((w2_ref, wb), (w3_ref, wc)):
        for d in range(4):
            for e in range(4):
                for par in range(2):
                    dst[pl.ds(d * 256 + e * 64, HID), pl.ds(par * LANES, LANES)] = (
                        0.5
                        * jnp.concatenate(
                            [tap(src, d - par, e), tap(src, d - par, e - 1)], axis=1
                        )
                    ).astype(BF16)
    wlast[...] = jnp.zeros_like(wlast)
    eye = jnp.where(
        lax.broadcasted_iota(jnp.int32, (HID, HID), 0)
        == lax.broadcasted_iota(jnp.int32, (HID, HID), 1),
        1.0,
        0.0,
    ).astype(BF16)
    for a in range(3):
        for e in range(3):
            wlast[a, e, :, pl.ds(0, F)] = lax.dot_general(
                eye, w4_ref[a, e], (((1,), (1,)), ((), ())), preferred_element_type=F32
            )
    for par in range(2):
        for e in range(4):
            for q in range(2):
                total = tap(wlast, par + 2, e - q)
                for o in range(1, 4):
                    if 0 <= par + 2 - o <= 2:
                        total = total + pltpu.roll(tap(wlast, par + 2 - o, e - q), 8 * o, 1)
                wd[pl.ds(par * 256 + e * 64, HID), pl.ds(q * LANES, LANES)] = total.astype(BF16)
    bias[...] = jnp.zeros_like(bias)
    for i, b_ref in enumerate((b1_ref, b2_ref, b3_ref)):
        b = 0.5 * b_ref[...]
        bias[pl.ds(i, 1), :] = jnp.concatenate([b, b, b, b], axis=1)
    for r in range(ROWS):
        bias[pl.ds(3, 1), pl.ds(8 * r, F)] = b4_ref[...]

    def body(t, carry):
        c = t - CHUNKS * (t // CHUNKS)

        @pl.when(t < CHUNKS - 1)
        def _():
            open_chunk(t + 1)

        done = compute(t, c)

        for i in range(LV):
            cur[LV * c + i] = done[i][0]
            prev[LV * c + i] = done[i][1]

        @pl.when(t < CHUNKS)
        def _():
            send_halos(t + CHUNKS, c)

        @pl.when(t >= CHUNKS)
        def _():
            for i in range(LV):
                l = LV * c + i
                advanced = cur[l]
                filtered = prev[l]
                zbuf[0] = jnp.where(is0, advanced, filtered)
                zbuf[1] = jnp.where(is0, filtered, advanced)
                for f in range(F):
                    snd[l, f] = zbuf[1, pl.ds(f, ROWS, stride=8), :]
                    out[0, HALF * g + l, f] = zbuf[0, pl.ds(f, ROWS, stride=8), :]
            final_copy(c, g).start()

        return carry

    lax.fori_loop(0, STEPS * CHUNKS, body, 0)

    for c in range(CHUNKS):
        tile_copy(c).wait_send()
        final_copy(c, g).wait_send()

    def drain(t, carry):
        for k in range(8):
            halo_copy(t, k).wait_send()
        return carry

    lax.fori_loop(0, STEPS * CHUNKS, drain, 0)
    for c in range(CHUNKS):
        final_copy(c, 1 - g).wait_recv()


def solution(mesh):
    nrow = mesh.shape["row"]
    ncol = mesh.shape["col"]

    def shards(fields, sea_mask, column_levels, w1, b1, w2, b2, w3, b3, w4, b4):
        vmem = pl.BlockSpec(memory_space=pltpu.VMEM)
        hbm = pl.BlockSpec(memory_space=pltpu.HBM)
        count = STEPS * CHUNKS
        operands = (
            fields,
            sea_mask,
            column_levels,
            w1,
            b1.reshape(1, -1),
            w2,
            b2.reshape(1, -1),
            w3,
            b3.reshape(1, -1),
            jnp.transpose(w4, (0, 1, 3, 2)),
            b4.reshape(1, -1),
        )
        dma = pltpu.SemaphoreType.DMA
        operands = tuple(pltpu.with_memory_space_constraint(x, pltpu.HBM) for x in operands)
        return pl.pallas_call(
            functools.partial(kernel, nrow, ncol),
            out_shape=jax.ShapeDtypeStruct(fields.shape, F32),
            in_specs=[hbm] * len(operands),
            out_specs=vmem,
            scratch_shapes=[
                pltpu.VMEM((HALF, F, ROWS, LANES), F32),
                *[pltpu.VMEM(x.shape, x.dtype) for x in operands[1:]],
                pltpu.VMEM((HALF, F, ROWS, LANES), F32),
                pltpu.VMEM((HALF, RF, LANES), F32),
                pltpu.VMEM((HALF, RF, LANES), F32),
                pltpu.VMEM((RF, LANES), F32),
                pltpu.VMEM((RF, LANES), F32),
                pltpu.VMEM((count, LV, 48, LANES), BF16),
                pltpu.VMEM((count, LV, 48, LANES), BF16),
                pltpu.VMEM((count, 3 * 8 * LV, LANES), BF16),
                pltpu.VMEM((count, 2, LV, 48, LANES), BF16),
                pltpu.VMEM((count, 2, 3 * 8 * LV, LANES), BF16),
                pltpu.VMEM((count, 4, 8 * LV, LANES), BF16),
                pltpu.VMEM((8 * TILES, 256), BF16),
                pltpu.VMEM((128, 256), BF16),
                pltpu.VMEM((1024, 256), BF16),
                pltpu.VMEM((1024, 256), BF16),
                pltpu.VMEM((512, 256), BF16),
                pltpu.VMEM((128, 256), F32),
                pltpu.VMEM((3, 3, HID, LANES), F32),
                pltpu.VMEM((8, 256), F32),
                pltpu.VMEM((LV, 4, 192, 256), BF16),
                pltpu.VMEM((11, WIDE, LANES), BF16),
                *[pltpu.VMEM((n, WIDE + 16, LANES), BF16) for n in (11, 11, 10, 10, 9, 9)],
                pltpu.VMEM((LV, 16 * TILES, LANES), F32),
                pltpu.VMEM((LV, RF, LANES), F32),
                pltpu.VMEM((2, RF, LANES), F32),
                pltpu.VMEM((HALF, F, ROWS, LANES), F32),
                dma((11,)),
                dma((CHUNKS,)),
                dma((CHUNKS,)),
                dma((CHUNKS,)),
                dma((CHUNKS,)),
                dma((count, 8)),
                dma((count, 8)),
            ],
            compiler_params=pltpu.CompilerParams(
                collective_id=0,
                has_side_effects=True,
                vmem_limit_bytes=24 << 20,
            ),
        )(*operands)

    return jax.shard_map(
        shards,
        mesh=mesh,
        in_specs=(P("grp", None, None, "row", "col"), P("row", "col"), P("row", "col")) + (P(),) * 8,
        out_specs=P("grp", None, None, "row", "col"),
        check_vma=False,
    )
```

```python
import functools

import jax
import jax.numpy as jnp
from jax import lax
from jax.experimental import pallas as pl
from jax.experimental.pallas import tpu as pltpu
from jax.sharding import PartitionSpec as P

COURANT = 0.25
FORCE_STEP = 0.5
CORIOLIS = 0.2
ASSELIN = 0.1
F32 = jnp.float32
BF16 = jnp.bfloat16
MESH = pl.DeviceIdType.MESH

F = 6
HID = 64
LANES = 128
ROWS = 16
TILES = 9
WIDE = 16 * TILES
HALF = 4
LV = 2
CHUNKS = HALF // LV
STEPS = 2
RF = ROWS * 8

DIRS = ((1, 0), (-1, 0), (0, 1), (0, -1), (1, 1), (1, -1), (-1, 1), (-1, -1))
OPP = (1, 0, 3, 2, 7, 6, 5, 4)
N_, S_, E_, W_, NE_, NW_, SE_, SW_ = range(8)

BLOCKS = ((0, 0, 2), (0, 2, 2), (0, 4, 2), (0, 6, 2), (0, 8, 2), (0, 10, 1), (1, 0, 3), (1, 3, 2), (1, 5, 3), (1, 8, 2), (2, 0, 2), (2, 2, 2), (2, 4, 3), (2, 7, 2), (3, 0, 4), (3, 4, 3), (3, 7, 2))
LAG = 2

SOUTH = (((0, 0), (0, 1), (1, 0)), ((0, 0), (0, 1)), ((0, 0),))
NORTH = (((9, 1), (10, 0), (10, 1)), ((9, 0), (9, 1)), ((8, 1),))

GELU_TYPE = BF16
K1 = 2.0 * 0.7978845608028654
K2 = 8.0 * 0.7978845608028654 * 0.044715


def gelu_of_half(h):
    inner = h * (h * h * K2 + K1)
    return h * jnp.tanh(inner) + h


def kernel(
    nrow,
    ncol,
    fields,
    mask_hbm,
    levels_hbm,
    w1_hbm,
    b1_hbm,
    w2_hbm,
    b2_hbm,
    w3_hbm,
    b3_hbm,
    w4_hbm,
    b4_hbm,
    out,
    mine,
    mask_ref,
    levels_ref,
    w1_ref,
    b1_ref,
    w2_ref,
    b2_ref,
    w3_ref,
    b3_ref,
    w4_ref,
    b4_ref,
    other,
    cur,
    prev,
    depth,
    coriolis,
    stage_n,
    stage_s,
    stage_p,
    halo,
    pack_side,
    pack_diag,
    sel,
    wa,
    wb,
    wc,
    wd,
    wtmp,
    wlast,
    bias,
    xb,
    lhs,
    f1e,
    f1o,
    f2e,
    f2o,
    f3e,
    f3o,
    spread,
    moved,
    zbuf,
    snd,
    load_s,
    tile_ss,
    tile_rs,
    fin_ss,
    fin_rs,
    halo_ss,
    halo_rs,
):
    g = lax.axis_index("grp")
    ri = lax.axis_index("row")
    ci = lax.axis_index("col")
    is0 = g == 0
    partner = {"grp": 1 - g}

    def peer(k):
        dr, dc = DIRS[k]
        where = {}
        if dr:
            where["row"] = lax.rem(ri + dr + nrow, nrow)
        if dc:
            where["col"] = lax.rem(ci + dc + ncol, ncol)
        return where

    barrier = pltpu.get_barrier_semaphore()
    for k in range(8):
        pl.semaphore_signal(barrier, inc=1, device_id=peer(k), device_id_type=MESH)
    pl.semaphore_signal(barrier, inc=1, device_id=partner, device_id_type=MESH)

    loads = [
        pltpu.make_async_copy(src, dst, load_s.at[i])
        for i, (src, dst) in enumerate(
            (
                (mask_hbm, mask_ref),
                (levels_hbm, levels_ref),
                (w1_hbm, w1_ref),
                (b1_hbm, b1_ref),
                (b2_hbm, b2_ref),
                (b3_hbm, b3_ref),
                (b4_hbm, b4_ref),
                (w2_hbm, w2_ref),
                (w3_hbm, w3_ref),
                (w4_hbm, w4_ref),
                (fields.at[0, pl.ds(HALF * g, HALF)], mine),
            )
        )
    ]
    for load in loads:
        load.start()

    pl.semaphore_wait(barrier, 9)

    def tile_copy(c):
        return pltpu.make_async_remote_copy(
            src_ref=fields.at[0, pl.ds(HALF * (1 - g) + LV * c, LV)],
            dst_ref=other.at[pl.ds(LV * c, LV)],
            send_sem=tile_ss.at[c],
            recv_sem=tile_rs.at[c],
            device_id=partner,
            device_id_type=MESH,
        )

    def final_copy(c, owner):
        return pltpu.make_async_remote_copy(
            src_ref=snd.at[pl.ds(LV * c, LV)],
            dst_ref=out.at[0, pl.ds(HALF * owner + LV * c, LV)],
            send_sem=fin_ss.at[c],
            recv_sem=fin_rs.at[c],
            device_id=partner,
            device_id_type=MESH,
        )

    def halo_copy(t, k):
        if k < 2:
            src = (stage_n if k == N_ else stage_s).at[t]
            dst = halo.at[t, OPP[k]]
        elif k < 4:
            src = stage_p.at[t]
            dst = pack_side.at[t, OPP[k] - 2]
        else:
            src = stage_p.at[t, pl.ds(0, 8 * LV)]
            dst = pack_diag.at[t, OPP[k] - 4]
        return pltpu.make_async_remote_copy(
            src_ref=src,
            dst_ref=dst,
            send_sem=halo_ss.at[t, k],
            recv_sem=halo_rs.at[t, OPP[k]],
            device_id=peer(k),
            device_id_type=MESH,
        )

    tile_copy(0).start()
    for load in loads:
        load.wait()

    lev = jnp.where(mask_ref[...] > 0, levels_ref[...], 0).astype(F32)
    for r in range(ROWS):
        depth[pl.ds(8 * r, 8), :] = jnp.broadcast_to(lev[r : r + 1, :], (8, LANES))
    rows_of = lax.broadcasted_iota(jnp.int32, (RF, LANES), 0)
    lat = (rows_of // 8 + ri * ROWS).astype(F32)
    field_of = rows_of % 8
    sine = CORIOLIS * jnp.sin(jnp.pi * (lat + 0.5) / (nrow * ROWS) - 0.5 * jnp.pi)
    coriolis[...] = jnp.where(field_of == 0, sine, jnp.where(field_of == 1, -sine, 0.0))
    cur[...] = jnp.zeros_like(cur)
    prev[...] = jnp.zeros_like(prev)
    m_of = lax.broadcasted_iota(jnp.int32, (8 * TILES + 8, 256), 0)
    j_of = lax.broadcasted_iota(jnp.int32, (8 * TILES + 8, 256), 1)
    pair_of = TILES * (m_of % 8) + m_of // 8
    sel[...] = jnp.where(j_of == (2 * pair_of + 252) % 256, 1.0, 0.0).astype(BF16)

    lane8 = lax.broadcasted_iota(jnp.int32, (8, LANES), 1)
    south_open = jnp.where(ri > 0, 1.0, 0.0).astype(F32)
    north_open = jnp.where(ri < nrow - 1, 1.0, 0.0).astype(F32)

    def masked_state(l):
        wet = (HALF * g + l).astype(F32) < depth[...]
        p = jnp.where(wet, prev[l], 0.0).astype(BF16).astype(F32)
        m = jnp.where(wet, cur[l], 0.0)
        return wet, p, m

    def packed(x):
        total = jnp.zeros((8, LANES), F32)
        for r in range(ROWS):
            part = pltpu.roll(x[8 * r : 8 * r + 8, :], (4 + 8 * r) % LANES, 1)
            total = jnp.where(lane8 // 8 == r, part, total)
        return total

    def halves(x):
        high = x.astype(BF16).astype(F32)
        return high, x - high

    def send_halos(t, c):
        rows = [[], [], []]
        for i in range(LV):
            _, p, m = masked_state(LV * c + i)
            stage_n[t, i, pl.ds(0, 32), :] = p[96:128, :].astype(BF16)
            stage_n[t, i, pl.ds(32, 16), :] = jnp.concatenate(
                halves(m[120:128, :]), axis=0
            ).astype(BF16)
            stage_s[t, i, pl.ds(0, 32), :] = p[0:32, :].astype(BF16)
            stage_s[t, i, pl.ds(32, 16), :] = jnp.concatenate(halves(m[0:8, :]), axis=0).astype(
                BF16
            )
            rows[0].append(packed(p))
            high, low = halves(packed(m))
            rows[1].append(high)
            rows[2].append(low)
        for j in range(3):
            stage_p[t, pl.ds(8 * LV * j, 8 * LV), :] = jnp.concatenate(rows[j], axis=0).astype(BF16)
        for k in range(8):
            halo_copy(t, k).start()

    def side(t, k, i, j):
        if k < 4:
            part = pack_side[t, k - 2, pl.ds(8 * LV * j, 8 * LV), :]
        else:
            part = pack_diag[t, k - 4]
        return part.astype(F32)[8 * i : 8 * i + 8, :]

    def edge_row(t, k, i):
        part = halo[t, k, i, pl.ds(32, 16), :].astype(F32)
        return part[0:8, :] + part[8:16, :]

    def open_chunk(c):
        tile_copy(c).wait_recv()
        for i in range(LV):
            l = LV * c + i
            for f in range(F):
                own = mine[l, f]
                oth = other[l, f]
                cur[l, pl.ds(f, ROWS, stride=8), :] = jnp.where(is0, own, oth)
                prev[l, pl.ds(f, ROWS, stride=8), :] = jnp.where(is0, oth, own)
        send_halos(c, c)

    def fill_lhs(t, both):
        for i in range(LV):
            p = both[i][1]
            first = lane8 % 8 < 4
            mid, south, north = [
                jnp.where(first, side(t, w, i, 0), side(t, e, i, 0))
                for w, e in ((W_, E_), (SW_, SE_), (NW_, NE_))
            ]
            south = south * south_open
            north = north * north_open
            low = halo[t, S_, i, pl.ds(0, 32), :].astype(F32)
            high = halo[t, N_, i, pl.ds(0, 32), :].astype(F32)
            xm = jnp.concatenate([low * south_open, p, high * north_open], axis=0)
            xh = jnp.concatenate(
                [pltpu.roll(south, (124 - 8 * (12 + j)) % LANES, 1) for j in range(4)]
                + [pltpu.roll(mid, (124 - 8 * j) % LANES, 1) for j in range(ROWS)]
                + [pltpu.roll(north, (124 - 8 * j) % LANES, 1) for j in range(4)],
                axis=0,
            )
            lane = lax.broadcasted_iota(jnp.int32, (192, LANES), 1)
            for e in range(2):
                if e == 0:
                    a, b = xm, xh
                else:
                    ra = pltpu.roll(xm, LANES - e, 1)
                    rb = pltpu.roll(xh, LANES - e, 1)
                    keep = lane < LANES - e
                    a, b = jnp.where(keep, ra, rb), jnp.where(keep, rb, ra)
                xb[i, e, :, pl.ds(0, LANES)] = a.astype(BF16)
                xb[i, e, :, pl.ds(LANES, LANES)] = b.astype(BF16)
        for n, group in enumerate(((0, 2, 1, 3), (4, 6, 5, 7), (8, 10, 9, 9))):
            got = []
            for i in range(LV):
                window = jnp.concatenate(
                    [xb[i, e, pl.ds(16 * r, 32), :] for r in group for e in range(2)], axis=0
                )
                got.append(
                    lax.dot_general(
                        sel[...], window, (((1,), (1,)), ((), ())), preferred_element_type=F32
                    ).reshape(TILES + 1, 1, 8, 256)
                )
            merged = jnp.concatenate(got, axis=1).reshape(WIDE + 16, 256).astype(BF16)
            for j in range(2):
                lhs[2 * n + j] = merged[:, j * LANES : (j + 1) * LANES]

    stores = ((f1e, f1o), (f2e, f2o), (f3e, f3o))
    weights = (wa, wb, wc, wd)

    def block_dot(layer, r0, n):
        if layer == 0:
            at = (r0 // 4) * 2
            x = jnp.concatenate(
                [
                    lhs[pl.ds(at, n), pl.ds(16 * shift, WIDE), :].reshape(n * WIDE, LANES)
                    for shift in range(2)
                ],
                axis=1,
            )
            return jnp.dot(x, wa[(r0 // 2) % 2], preferred_element_type=F32)
        elif layer == 3:
            x = jnp.concatenate(
                [
                    src[pl.ds(r0, n), pl.ds(16 * shift, WIDE), :].reshape(n * WIDE, LANES)
                    for src in stores[2]
                    for shift in range(2)
                ],
                axis=1,
            )
        else:
            pieces = []
            for d in range(4):
                src = stores[layer - 1][d % 2]
                for shift in range(2):
                    pieces.append(
                        src[pl.ds(r0 + d // 2, n), pl.ds(16 * shift, WIDE), :].reshape(
                            n * WIDE, LANES
                        )
                    )
            x = jnp.concatenate(pieces, axis=1)
        return jnp.dot(x, weights[layer][...], preferred_element_type=F32)

    def block_store(layer, r0, n, y, sums):
        if layer == 3:
            lanes = lax.broadcasted_iota(jnp.int32, (WIDE, LANES), 1)
            for i in range(n):
                r = r0 + i
                for q in range(2):
                    part = y[i * WIDE : (i + 1) * WIDE, q * LANES : (q + 1) * LANES]
                    if r == 0:
                        part = jnp.where(lanes >= 16, part, 0.0)
                    if r == ROWS // 2:
                        part = jnp.where(lanes < 16, part, 0.0)
                    if r != 1:
                        part = pltpu.roll(part, (16 * (r - 1)) % LANES, 1)
                    sums[q] = part if sums[q] is None else sums[q] + part
            return
        y = y + bias[pl.ds(layer, 1), :]
        h = gelu_of_half(y.astype(GELU_TYPE))
        for par in range(2):
            dst = stores[layer][par]
            for i in range(n):
                piece = h[i * WIDE : (i + 1) * WIDE, par * LANES : (par + 1) * LANES]
                if (r0 + i, par) in SOUTH[layer]:
                    piece = piece * south_open.astype(GELU_TYPE)
                if (r0 + i, par) in NORTH[layer]:
                    piece = piece * north_open.astype(GELU_TYPE)
                dst[r0 + i, pl.ds(0, WIDE), :] = piece.astype(BF16)
                edge = piece[0:16, :].astype(F32)
                edge = jnp.concatenate(
                    [pltpu.roll(edge[0:8], 7, 0), pltpu.roll(edge[8:16], 7, 0)], axis=0
                )
                dst[r0 + i, pl.ds(WIDE, 16), :] = edge.astype(BF16)

    def tendency(t, i, m):
        first = lane8 % 8 < 4
        m3 = m.reshape(ROWS, 8, LANES)
        msouth = edge_row(t, S_, i)
        mnorth = edge_row(t, N_, i)
        mmid = jnp.where(
            first,
            side(t, W_, i, 1) + side(t, W_, i, 2),
            side(t, E_, i, 1) + side(t, E_, i, 2),
        )
        mside = jnp.concatenate(
            [pltpu.roll(mmid, (124 - 8 * j) % LANES, 1) for j in range(ROWS)], axis=0
        )
        lane_rf = lax.broadcasted_iota(jnp.int32, (RF, LANES), 1)
        east = jnp.where(
            lane_rf == LANES - 1, pltpu.roll(mside, LANES - 1, 1), pltpu.roll(m, LANES - 1, 1)
        ).reshape(ROWS, 8, LANES)
        west = jnp.where(lane_rf == 0, pltpu.roll(mside, 1, 1), pltpu.roll(m, 1, 1)).reshape(
            ROWS, 8, LANES
        )
        u = jnp.broadcast_to(m3[:, 0:1, :], m3.shape)
        v = jnp.broadcast_to(m3[:, 1:2, :], m3.shape)
        flux_east = (u + east[:, 0:1, :]) * (m3 + east)
        flux_west = (west[:, 0:1, :] + u) * (west + m3)
        ext = jnp.concatenate([msouth[None], m3, mnorth[None]], axis=0)
        vext = jnp.broadcast_to(ext[:, 1:2, :], ext.shape)
        flux = (vext[:-1] + vext[1:]) * (ext[:-1] + ext[1:])
        flux = jnp.concatenate(
            [flux[0:1] * south_open, flux[1:ROWS], flux[ROWS : ROWS + 1] * north_open], axis=0
        )
        spread_of = flux_east - flux_west + flux[1:] - flux[:-1]
        turn = jnp.where(
            lax.broadcasted_iota(jnp.int32, m3.shape, 1) == 0, v, u
        ) * coriolis[...].reshape(ROWS, 8, LANES)
        return (turn - (0.25 * COURANT) * spread_of).reshape(RF, LANES)

    def compute(t, c):
        for k in range(8):
            halo_copy(t, k).wait_recv()
        both = [masked_state(LV * c + i) for i in range(LV)]
        fill_lhs(t, both)
        sums = [None, None]
        waiting = []
        for n, block in enumerate(BLOCKS):
            y = block_dot(*block)
            waiting.append((*block, y))
            if len(waiting) > LAG:
                block_store(*waiting.pop(0), sums)
            if n in (5, 9):
                i = (5, 9).index(n)
                moved[i] = prev[LV * c + i] + tendency(t, i, both[i][2])
        for item in waiting:
            block_store(*item, sums)
        for q in range(2):
            total = (sums[q] + bias[pl.ds(3, 1), pl.ds(0, LANES)]).astype(BF16).astype(F32)
            for p in range(TILES):
                for i in range(LV):
                    at = 16 * p + 8 * i
                    spread[i, pl.ds(2 * p + q, 8, stride=2 * TILES), :] = total[at : at + 8, :]
        done = []
        for i in range(LV):
            wet = both[i][0]
            forcing = spread[i, pl.ds(0, LANES), :].T
            pv = prev[LV * c + i]
            cr = cur[LV * c + i]
            advanced = jnp.where(wet, moved[i] + FORCE_STEP * forcing, 0.0)
            filtered = cr + ASSELIN * (pv - 2.0 * cr + advanced)
            done.append((advanced, filtered))
        return done

    tile_copy(0).wait_send()
    for c in range(1, CHUNKS):
        tile_copy(c).start()
    open_chunk(0)

    def tap(ref, a, e):
        if 0 <= a <= 2 and 0 <= e <= 2:
            return ref[a, e].astype(F32)
        return jnp.zeros(ref.shape[2:], F32)

    wtmp[...] = jnp.zeros_like(wtmp)
    for e in range(4):
        for d in range(4):
            for par in range(2):
                both = 0.5 * jnp.concatenate(
                    [tap(w1_ref, d - par, e), tap(w1_ref, d - par, e - 1)], axis=1
                )
                for h in range(2):
                    at = (e // 2) * LANES + h * 64 + (e % 2) * 32 + d * 8
                    wtmp[h, pl.ds(at, F), pl.ds(par * LANES, LANES)] = both
    wa[...] = wtmp[...].astype(BF16)
    for src, dst in ((w2_ref, wb), (w3_ref, wc)):
        for d in range(4):
            for e in range(4):
                for par in range(2):
                    dst[pl.ds(d * 256 + e * 64, HID), pl.ds(par * LANES, LANES)] = (
                        0.5
                        * jnp.concatenate(
                            [tap(src, d - par, e), tap(src, d - par, e - 1)], axis=1
                        )
                    ).astype(BF16)
    wlast[...] = jnp.zeros_like(wlast)
    eye = jnp.where(
        lax.broadcasted_iota(jnp.int32, (HID, HID), 0)
        == lax.broadcasted_iota(jnp.int32, (HID, HID), 1),
        1.0,
        0.0,
    ).astype(BF16)
    for a in range(3):
        for e in range(3):
            wlast[a, e, :, pl.ds(0, F)] = lax.dot_general(
                eye, w4_ref[a, e], (((1,), (1,)), ((), ())), preferred_element_type=F32
            )
    for par in range(2):
        for e in range(4):
            for q in range(2):
                total = tap(wlast, par + 2, e - q)
                for o in range(1, 4):
                    if 0 <= par + 2 - o <= 2:
                        total = total + pltpu.roll(tap(wlast, par + 2 - o, e - q), 8 * o, 1)
                wd[pl.ds(par * 256 + e * 64, HID), pl.ds(q * LANES, LANES)] = total.astype(BF16)
    bias[...] = jnp.zeros_like(bias)
    for i, b_ref in enumerate((b1_ref, b2_ref, b3_ref)):
        b = 0.5 * b_ref[...]
        bias[pl.ds(i, 1), :] = jnp.concatenate([b, b, b, b], axis=1)
    for r in range(ROWS):
        bias[pl.ds(3, 1), pl.ds(8 * r, F)] = b4_ref[...]

    def body(t, carry):
        c = t - CHUNKS * (t // CHUNKS)

        @pl.when(t < CHUNKS - 1)
        def _():
            open_chunk(t + 1)

        done = compute(t, c)

        for i in range(LV):
            cur[LV * c + i] = done[i][0]
            prev[LV * c + i] = done[i][1]

        @pl.when(t < CHUNKS)
        def _():
            send_halos(t + CHUNKS, c)

        @pl.when(t >= CHUNKS)
        def _():
            for i in range(LV):
                l = LV * c + i
                advanced = cur[l]
                filtered = prev[l]
                zbuf[i] = jnp.where(is0, filtered, advanced)
                for f in range(F):
                    snd[l, f] = zbuf[i, pl.ds(f, ROWS, stride=8), :]
            final_copy(c, g).start()
            for i in range(LV):
                l = LV * c + i
                zbuf[i] = jnp.where(is0, cur[l], prev[l])
                for f in range(F):
                    out[0, HALF * g + l, f] = zbuf[i, pl.ds(f, ROWS, stride=8), :]

        return carry

    lax.fori_loop(0, STEPS * CHUNKS, body, 0)

    for c in range(1, CHUNKS):
        tile_copy(c).wait_send()
    for c in range(CHUNKS):
        final_copy(c, g).wait_send()

    def drain(t, carry):
        for k in range(8):
            halo_copy(t, k).wait_send()
        return carry

    lax.fori_loop(0, STEPS * CHUNKS, drain, 0)
    for c in range(CHUNKS):
        final_copy(c, 1 - g).wait_recv()


def solution(mesh):
    nrow = mesh.shape["row"]
    ncol = mesh.shape["col"]

    def shards(fields, sea_mask, column_levels, w1, b1, w2, b2, w3, b3, w4, b4):
        vmem = pl.BlockSpec(memory_space=pltpu.VMEM)
        hbm = pl.BlockSpec(memory_space=pltpu.HBM)
        count = STEPS * CHUNKS
        operands = (
            fields,
            sea_mask,
            column_levels,
            w1,
            b1.reshape(1, -1),
            w2,
            b2.reshape(1, -1),
            w3,
            b3.reshape(1, -1),
            jnp.transpose(w4, (0, 1, 3, 2)),
            b4.reshape(1, -1),
        )
        dma = pltpu.SemaphoreType.DMA
        operands = tuple(pltpu.with_memory_space_constraint(x, pltpu.HBM) for x in operands)
        return pl.pallas_call(
            functools.partial(kernel, nrow, ncol),
            out_shape=jax.ShapeDtypeStruct(fields.shape, F32),
            in_specs=[hbm] * len(operands),
            out_specs=vmem,
            scratch_shapes=[
                pltpu.VMEM((HALF, F, ROWS, LANES), F32),
                *[pltpu.VMEM(x.shape, x.dtype) for x in operands[1:]],
                pltpu.VMEM((HALF, F, ROWS, LANES), F32),
                pltpu.VMEM((HALF, RF, LANES), F32),
                pltpu.VMEM((HALF, RF, LANES), F32),
                pltpu.VMEM((RF, LANES), F32),
                pltpu.VMEM((RF, LANES), F32),
                pltpu.VMEM((count, LV, 48, LANES), BF16),
                pltpu.VMEM((count, LV, 48, LANES), BF16),
                pltpu.VMEM((count, 3 * 8 * LV, LANES), BF16),
                pltpu.VMEM((count, 2, LV, 48, LANES), BF16),
                pltpu.VMEM((count, 2, 3 * 8 * LV, LANES), BF16),
                pltpu.VMEM((count, 4, 8 * LV, LANES), BF16),
                pltpu.VMEM((8 * TILES + 8, 256), BF16),
                pltpu.VMEM((2, 256, 256), BF16),
                pltpu.VMEM((1024, 256), BF16),
                pltpu.VMEM((1024, 256), BF16),
                pltpu.VMEM((512, 256), BF16),
                pltpu.VMEM((2, 256, 256), F32),
                pltpu.VMEM((3, 3, HID, LANES), F32),
                pltpu.VMEM((8, 256), F32),
                pltpu.VMEM((LV, 2, 192, 256), BF16),
                pltpu.VMEM((6, WIDE + 16, LANES), BF16),
                *[pltpu.VMEM((n, WIDE + 16, LANES), BF16) for n in (11, 11, 10, 10, 9, 9)],
                pltpu.VMEM((LV, 16 * TILES, LANES), F32),
                pltpu.VMEM((LV, RF, LANES), F32),
                pltpu.VMEM((2, RF, LANES), F32),
                pltpu.VMEM((HALF, F, ROWS, LANES), F32),
                dma((11,)),
                dma((CHUNKS,)),
                dma((CHUNKS,)),
                dma((CHUNKS,)),
                dma((CHUNKS,)),
                dma((count, 8)),
                dma((count, 8)),
            ],
            compiler_params=pltpu.CompilerParams(
                collective_id=0,
                has_side_effects=True,
                vmem_limit_bytes=24 << 20,
            ),
        )(*operands)

    return jax.shard_map(
        shards,
        mesh=mesh,
        in_specs=(P("grp", None, None, "row", "col"), P("row", "col"), P("row", "col")) + (P(),) * 8,
        out_specs=P("grp", None, None, "row", "col"),
        check_vma=False,
    )
```

```python
import functools

import jax
import jax.numpy as jnp
from jax import lax
from jax.experimental import pallas as pl
from jax.experimental.pallas import tpu as pltpu
from jax.sharding import PartitionSpec as P

COURANT = 0.25
FORCE_STEP = 0.5
CORIOLIS = 0.2
ASSELIN = 0.1
F32 = jnp.float32
BF16 = jnp.bfloat16
MESH = pl.DeviceIdType.MESH

F = 6
HID = 64
LANES = 128
ROWS = 16
TILES = 9
WIDE = 16 * TILES
HALF = 4
LV = 2
CHUNKS = HALF // LV
STEPS = 2
RF = ROWS * 8

DIRS = ((1, 0), (-1, 0), (0, 1), (0, -1), (1, 1), (1, -1), (-1, 1), (-1, -1))
OPP = (1, 0, 3, 2, 7, 6, 5, 4)
N_, S_, E_, W_, NE_, NW_, SE_, SW_ = range(8)

BLOCKS = ((0, 0, 2), (0, 2, 2), (0, 4, 2), (0, 6, 2), (0, 8, 2), (0, 10, 1), (1, 0, 4), (1, 4, 4), (1, 8, 2), (2, 0, 3), (2, 3, 4), (2, 7, 2), (3, 0, 3), (3, 3, 4), (3, 7, 2))
LAG = 1

SOUTH = (((0, 0), (0, 1), (1, 0)), ((0, 0), (0, 1)), ((0, 0),))
NORTH = (((9, 1), (10, 0), (10, 1)), ((9, 0), (9, 1)), ((8, 1),))

GELU_TYPE = BF16
K1 = 2.0 * 0.7978845608028654
K2 = 8.0 * 0.7978845608028654 * 0.044715


def gelu_of_half(h):
    inner = h * (h * h * K2 + K1)
    return h * jnp.tanh(inner) + h


def kernel(
    nrow,
    ncol,
    fields,
    mask_hbm,
    levels_hbm,
    w1_hbm,
    b1_hbm,
    w2_hbm,
    b2_hbm,
    w3_hbm,
    b3_hbm,
    w4_hbm,
    b4_hbm,
    out,
    mine,
    mask_ref,
    levels_ref,
    w1_ref,
    b1_ref,
    w2_ref,
    b2_ref,
    w3_ref,
    b3_ref,
    w4_ref,
    b4_ref,
    other,
    cur,
    prev,
    depth,
    coriolis,
    stage_n,
    stage_s,
    stage_p,
    halo,
    pack_side,
    pack_diag,
    sel,
    wa,
    wb,
    wc,
    wd,
    wtmp,
    wlast,
    bias,
    xb,
    lhs,
    f1e,
    f1o,
    f2e,
    f2o,
    f3e,
    f3o,
    spread,
    moved,
    zbuf,
    snd,
    sems,
):
    g = lax.axis_index("grp")
    ri = lax.axis_index("row")
    ci = lax.axis_index("col")
    is0 = g == 0
    partner = {"grp": 1 - g}

    def peer(k):
        dr, dc = DIRS[k]
        where = {}
        if dr:
            where["row"] = lax.rem(ri + dr + nrow, nrow)
        if dc:
            where["col"] = lax.rem(ci + dc + ncol, ncol)
        return where

    barrier = pltpu.get_barrier_semaphore()
    for k in range(8):
        pl.semaphore_signal(barrier, inc=1, device_id=peer(k), device_id_type=MESH)
    pl.semaphore_signal(barrier, inc=1, device_id=partner, device_id_type=MESH)

    loads = [
        pltpu.make_async_copy(src, dst, sems.at[i])
        for i, (src, dst) in enumerate(
            (
                (mask_hbm, mask_ref),
                (levels_hbm, levels_ref),
                (w1_hbm, w1_ref),
                (b1_hbm, b1_ref),
                (b2_hbm, b2_ref),
                (b3_hbm, b3_ref),
                (b4_hbm, b4_ref),
                (w2_hbm, w2_ref),
                (w3_hbm, w3_ref),
                (w4_hbm, w4_ref),
                (fields.at[0, pl.ds(HALF * g, HALF)], mine),
            )
        )
    ]
    for load in loads:
        load.start()

    pl.semaphore_wait(barrier, 9)

    def tile_copy(c):
        return pltpu.make_async_remote_copy(
            src_ref=fields.at[0, pl.ds(HALF * (1 - g) + LV * c, LV)],
            dst_ref=other.at[pl.ds(LV * c, LV)],
            send_sem=sems.at[11 + c],
            recv_sem=sems.at[13 + c],
            device_id=partner,
            device_id_type=MESH,
        )

    def final_copy(c, owner):
        return pltpu.make_async_remote_copy(
            src_ref=snd.at[pl.ds(LV * c, LV)],
            dst_ref=out.at[0, pl.ds(HALF * owner + LV * c, LV)],
            send_sem=sems.at[15 + c],
            recv_sem=sems.at[17 + c],
            device_id=partner,
            device_id_type=MESH,
        )

    def halo_copy(t, k):
        if k < 2:
            src = (stage_n if k == N_ else stage_s).at[t]
            dst = halo.at[t, OPP[k]]
        elif k < 4:
            src = stage_p.at[t]
            dst = pack_side.at[t, OPP[k] - 2]
        else:
            src = stage_p.at[t, pl.ds(0, 8 * LV)]
            dst = pack_diag.at[t, OPP[k] - 4]
        return pltpu.make_async_remote_copy(
            src_ref=src,
            dst_ref=dst,
            send_sem=sems.at[19 + 8 * t + k],
            recv_sem=sems.at[51 + 8 * t + OPP[k]],
            device_id=peer(k),
            device_id_type=MESH,
        )

    tile_copy(0).start()
    for load in loads:
        load.wait()

    lev = jnp.where(mask_ref[...] > 0, levels_ref[...], 0).astype(F32)
    for r in range(ROWS):
        depth[pl.ds(8 * r, 8), :] = jnp.broadcast_to(lev[r : r + 1, :], (8, LANES))
    rows_of = lax.broadcasted_iota(jnp.int32, (RF, LANES), 0)
    lat = (rows_of // 8 + ri * ROWS).astype(F32)
    field_of = rows_of % 8
    sine = CORIOLIS * jnp.sin(jnp.pi * (lat + 0.5) / (nrow * ROWS) - 0.5 * jnp.pi)
    coriolis[...] = jnp.where(field_of == 0, sine, jnp.where(field_of == 1, -sine, 0.0))
    cur[...] = jnp.zeros_like(cur)
    prev[...] = jnp.zeros_like(prev)
    m_of = lax.broadcasted_iota(jnp.int32, (8 * TILES + 8, 256), 0)
    j_of = lax.broadcasted_iota(jnp.int32, (8 * TILES + 8, 256), 1)
    pair_of = TILES * (m_of % 8) + m_of // 8
    sel[...] = jnp.where(j_of == (2 * pair_of + 252) % 256, 1.0, 0.0).astype(BF16)

    lane8 = lax.broadcasted_iota(jnp.int32, (8, LANES), 1)
    south_open = jnp.where(ri > 0, 1.0, 0.0).astype(F32)
    north_open = jnp.where(ri < nrow - 1, 1.0, 0.0).astype(F32)

    def masked_state(l):
        wet = (HALF * g + l).astype(F32) < depth[...]
        p = jnp.where(wet, prev[l], 0.0).astype(BF16).astype(F32)
        m = jnp.where(wet, cur[l], 0.0)
        return wet, p, m

    def packed(x):
        total = jnp.zeros((8, LANES), F32)
        for r in range(ROWS):
            part = pltpu.roll(x[8 * r : 8 * r + 8, :], (4 + 8 * r) % LANES, 1)
            total = jnp.where(lane8 // 8 == r, part, total)
        return total

    def halves(x):
        high = x.astype(BF16).astype(F32)
        return high, x - high

    def send_halos(t, c):
        rows = [[], [], []]
        for i in range(LV):
            _, p, m = masked_state(LV * c + i)
            stage_n[t, i, pl.ds(0, 32), :] = p[96:128, :].astype(BF16)
            stage_n[t, i, pl.ds(32, 16), :] = jnp.concatenate(
                halves(m[120:128, :]), axis=0
            ).astype(BF16)
            stage_s[t, i, pl.ds(0, 32), :] = p[0:32, :].astype(BF16)
            stage_s[t, i, pl.ds(32, 16), :] = jnp.concatenate(halves(m[0:8, :]), axis=0).astype(
                BF16
            )
            rows[0].append(packed(p))
            high, low = halves(packed(m))
            rows[1].append(high)
            rows[2].append(low)
        for j in range(3):
            stage_p[t, pl.ds(8 * LV * j, 8 * LV), :] = jnp.concatenate(rows[j], axis=0).astype(BF16)
        for k in range(8):
            halo_copy(t, k).start()

    def side(t, k, i, j):
        if k < 4:
            part = pack_side[t, k - 2, pl.ds(8 * LV * j, 8 * LV), :]
        else:
            part = pack_diag[t, k - 4]
        return part.astype(F32)[8 * i : 8 * i + 8, :]

    def edge_row(t, k, i):
        part = halo[t, k, i, pl.ds(32, 16), :].astype(F32)
        return part[0:8, :] + part[8:16, :]

    def open_chunk(c):
        tile_copy(c).wait_recv()
        for i in range(LV):
            l = LV * c + i
            for f in range(F):
                own = mine[l, f]
                oth = other[l, f]
                cur[l, pl.ds(f, ROWS, stride=8), :] = jnp.where(is0, own, oth)
                prev[l, pl.ds(f, ROWS, stride=8), :] = jnp.where(is0, oth, own)
        send_halos(c, c)

    def fill_lhs(t, both):
        for i in range(LV):
            p = both[i][1]
            first = lane8 % 8 < 4
            mid, south, north = [
                jnp.where(first, side(t, w, i, 0), side(t, e, i, 0))
                for w, e in ((W_, E_), (SW_, SE_), (NW_, NE_))
            ]
            south = south * south_open
            north = north * north_open
            low = halo[t, S_, i, pl.ds(0, 32), :].astype(F32)
            high = halo[t, N_, i, pl.ds(0, 32), :].astype(F32)
            xm = jnp.concatenate([low * south_open, p, high * north_open], axis=0)
            xh = jnp.concatenate(
                [pltpu.roll(south, (124 - 8 * (12 + j)) % LANES, 1) for j in range(4)]
                + [pltpu.roll(mid, (124 - 8 * j) % LANES, 1) for j in range(ROWS)]
                + [pltpu.roll(north, (124 - 8 * j) % LANES, 1) for j in range(4)],
                axis=0,
            )
            lane = lax.broadcasted_iota(jnp.int32, (192, LANES), 1)
            for e in range(2):
                if e == 0:
                    a, b = xm, xh
                else:
                    ra = pltpu.roll(xm, LANES - e, 1)
                    rb = pltpu.roll(xh, LANES - e, 1)
                    keep = lane < LANES - e
                    a, b = jnp.where(keep, ra, rb), jnp.where(keep, rb, ra)
                xb[i, e, :, pl.ds(0, LANES)] = a.astype(BF16)
                xb[i, e, :, pl.ds(LANES, LANES)] = b.astype(BF16)
        for n, group in enumerate(((0, 2, 1, 3), (4, 6, 5, 7), (8, 10, 9, 9))):
            got = []
            for i in range(LV):
                window = jnp.concatenate(
                    [xb[i, e, pl.ds(16 * r, 32), :] for r in group for e in range(2)], axis=0
                )
                got.append(
                    lax.dot_general(
                        sel[...], window, (((1,), (1,)), ((), ())), preferred_element_type=F32
                    ).reshape(TILES + 1, 1, 8, 256)
                )
            merged = jnp.concatenate(got, axis=1).reshape(WIDE + 16, 256).astype(BF16)
            for j in range(2):
                lhs[2 * n + j] = merged[:, j * LANES : (j + 1) * LANES]

    stores = ((f1e, f1o), (f2e, f2o), (f3e, f3o))
    weights = (wa, wb, wc, wd)

    def block_dot(layer, r0, n):
        if layer == 0:
            at = (r0 // 4) * 2
            x = jnp.concatenate(
                [
                    lhs[pl.ds(at, n), pl.ds(16 * shift, WIDE), :].reshape(n * WIDE, LANES)
                    for shift in range(2)
                ],
                axis=1,
            )
            return jnp.dot(x, wa[(r0 // 2) % 2], preferred_element_type=F32)
        elif layer == 3:
            x = jnp.concatenate(
                [
                    src[pl.ds(r0, n), pl.ds(16 * shift, WIDE), :].reshape(n * WIDE, LANES)
                    for src in stores[2]
                    for shift in range(2)
                ],
                axis=1,
            )
        else:
            pieces = []
            for d in range(4):
                src = stores[layer - 1][d % 2]
                for shift in range(2):
                    pieces.append(
                        src[pl.ds(r0 + d // 2, n), pl.ds(16 * shift, WIDE), :].reshape(
                            n * WIDE, LANES
                        )
                    )
            x = jnp.concatenate(pieces, axis=1)
        return jnp.dot(x, weights[layer][...], preferred_element_type=F32)

    def block_store(layer, r0, n, y, sums):
        if layer == 3:
            lanes = lax.broadcasted_iota(jnp.int32, (WIDE, LANES), 1)
            for i in range(n):
                r = r0 + i
                for q in range(2):
                    part = y[i * WIDE : (i + 1) * WIDE, q * LANES : (q + 1) * LANES]
                    if r == 0:
                        part = jnp.where(lanes >= 16, part, 0.0)
                    if r == ROWS // 2:
                        part = jnp.where(lanes < 16, part, 0.0)
                    if r != 1:
                        part = pltpu.roll(part, (16 * (r - 1)) % LANES, 1)
                    sums[q] = part if sums[q] is None else sums[q] + part
            return
        y = y + bias[pl.ds(layer, 1), :]
        h = gelu_of_half(y.astype(GELU_TYPE))
        for par in range(2):
            dst = stores[layer][par]
            for i in range(n):
                piece = h[i * WIDE : (i + 1) * WIDE, par * LANES : (par + 1) * LANES]
                if (r0 + i, par) in SOUTH[layer]:
                    piece = piece * south_open.astype(GELU_TYPE)
                if (r0 + i, par) in NORTH[layer]:
                    piece = piece * north_open.astype(GELU_TYPE)
                dst[r0 + i, pl.ds(0, WIDE), :] = piece.astype(BF16)
                edge = piece[0:16, :].astype(F32)
                edge = jnp.concatenate(
                    [pltpu.roll(edge[0:8], 7, 0), pltpu.roll(edge[8:16], 7, 0)], axis=0
                )
                dst[r0 + i, pl.ds(WIDE, 16), :] = edge.astype(BF16)

    def tendency(t, i, m):
        first = lane8 % 8 < 4
        m3 = m.reshape(ROWS, 8, LANES)
        msouth = edge_row(t, S_, i)
        mnorth = edge_row(t, N_, i)
        mmid = jnp.where(
            first,
            side(t, W_, i, 1) + side(t, W_, i, 2),
            side(t, E_, i, 1) + side(t, E_, i, 2),
        )
        mside = jnp.concatenate(
            [pltpu.roll(mmid, (124 - 8 * j) % LANES, 1) for j in range(ROWS)], axis=0
        )
        lane_rf = lax.broadcasted_iota(jnp.int32, (RF, LANES), 1)
        east = jnp.where(
            lane_rf == LANES - 1, pltpu.roll(mside, LANES - 1, 1), pltpu.roll(m, LANES - 1, 1)
        ).reshape(ROWS, 8, LANES)
        west = jnp.where(lane_rf == 0, pltpu.roll(mside, 1, 1), pltpu.roll(m, 1, 1)).reshape(
            ROWS, 8, LANES
        )
        u = jnp.broadcast_to(m3[:, 0:1, :], m3.shape)
        v = jnp.broadcast_to(m3[:, 1:2, :], m3.shape)
        flux_east = (u + east[:, 0:1, :]) * (m3 + east)
        flux_west = (west[:, 0:1, :] + u) * (west + m3)
        ext = jnp.concatenate([msouth[None], m3, mnorth[None]], axis=0)
        vext = jnp.broadcast_to(ext[:, 1:2, :], ext.shape)
        flux = (vext[:-1] + vext[1:]) * (ext[:-1] + ext[1:])
        flux = jnp.concatenate(
            [flux[0:1] * south_open, flux[1:ROWS], flux[ROWS : ROWS + 1] * north_open], axis=0
        )
        spread_of = flux_east - flux_west + flux[1:] - flux[:-1]
        turn = jnp.where(
            lax.broadcasted_iota(jnp.int32, m3.shape, 1) == 0, v, u
        ) * coriolis[...].reshape(ROWS, 8, LANES)
        return (turn - (0.25 * COURANT) * spread_of).reshape(RF, LANES)

    def compute(t, c):
        for k in range(8):
            halo_copy(t, k).wait_recv()
        both = [masked_state(LV * c + i) for i in range(LV)]
        fill_lhs(t, both)
        sums = [None, None]
        waiting = []
        for n, block in enumerate(BLOCKS):
            y = block_dot(*block)
            waiting.append((*block, y))
            if len(waiting) > LAG:
                block_store(*waiting.pop(0), sums)
            if n in (5, 9):
                i = (5, 9).index(n)
                moved[i] = prev[LV * c + i] + tendency(t, i, both[i][2])
        for item in waiting:
            block_store(*item, sums)
        for q in range(2):
            total = (sums[q] + bias[pl.ds(3, 1), pl.ds(0, LANES)]).astype(BF16).astype(F32)
            for p in range(TILES):
                for i in range(LV):
                    at = 16 * p + 8 * i
                    spread[i, pl.ds(2 * p + q, 8, stride=2 * TILES), :] = total[at : at + 8, :]
        done = []
        for i in range(LV):
            wet = both[i][0]
            forcing = spread[i, pl.ds(0, LANES), :].T
            pv = prev[LV * c + i]
            cr = cur[LV * c + i]
            advanced = jnp.where(wet, moved[i] + FORCE_STEP * forcing, 0.0)
            filtered = cr + ASSELIN * (pv - 2.0 * cr + advanced)
            done.append((advanced, filtered))
        return done

    tile_copy(0).wait_send()
    for c in range(1, CHUNKS):
        tile_copy(c).start()
    open_chunk(0)

    def tap(ref, a, e):
        if 0 <= a <= 2 and 0 <= e <= 2:
            return ref[a, e].astype(F32)
        return jnp.zeros(ref.shape[2:], F32)

    wtmp[...] = jnp.zeros_like(wtmp)
    for e in range(4):
        for d in range(4):
            for par in range(2):
                both = 0.5 * jnp.concatenate(
                    [tap(w1_ref, d - par, e), tap(w1_ref, d - par, e - 1)], axis=1
                )
                for h in range(2):
                    at = (e // 2) * LANES + h * 64 + (e % 2) * 32 + d * 8
                    wtmp[h, pl.ds(at, F), pl.ds(par * LANES, LANES)] = both
    wa[...] = wtmp[...].astype(BF16)
    for src, dst in ((w2_ref, wb), (w3_ref, wc)):
        for d in range(4):
            for e in range(4):
                for par in range(2):
                    dst[pl.ds(d * 256 + e * 64, HID), pl.ds(par * LANES, LANES)] = (
                        0.5
                        * jnp.concatenate(
                            [tap(src, d - par, e), tap(src, d - par, e - 1)], axis=1
                        )
                    ).astype(BF16)
    wlast[...] = jnp.zeros_like(wlast)
    eye = jnp.where(
        lax.broadcasted_iota(jnp.int32, (HID, HID), 0)
        == lax.broadcasted_iota(jnp.int32, (HID, HID), 1),
        1.0,
        0.0,
    ).astype(BF16)
    for a in range(3):
        for e in range(3):
            wlast[a, e, :, pl.ds(0, F)] = lax.dot_general(
                eye, w4_ref[a, e], (((1,), (1,)), ((), ())), preferred_element_type=F32
            )
    for par in range(2):
        for e in range(4):
            for q in range(2):
                total = tap(wlast, par + 2, e - q)
                for o in range(1, 4):
                    if 0 <= par + 2 - o <= 2:
                        total = total + pltpu.roll(tap(wlast, par + 2 - o, e - q), 8 * o, 1)
                wd[pl.ds(par * 256 + e * 64, HID), pl.ds(q * LANES, LANES)] = total.astype(BF16)
    bias[...] = jnp.zeros_like(bias)
    for i, b_ref in enumerate((b1_ref, b2_ref, b3_ref)):
        b = 0.5 * b_ref[...]
        bias[pl.ds(i, 1), :] = jnp.concatenate([b, b, b, b], axis=1)
    for r in range(ROWS):
        bias[pl.ds(3, 1), pl.ds(8 * r, F)] = b4_ref[...]

    def body(t, carry):
        c = t - CHUNKS * (t // CHUNKS)

        @pl.when(t < CHUNKS - 1)
        def _():
            open_chunk(t + 1)

        done = compute(t, c)

        for i in range(LV):
            cur[LV * c + i] = done[i][0]
            prev[LV * c + i] = done[i][1]

        @pl.when(t < CHUNKS)
        def _():
            send_halos(t + CHUNKS, c)

        @pl.when(t >= CHUNKS)
        def _():
            for i in range(LV):
                l = LV * c + i
                advanced = cur[l]
                filtered = prev[l]
                zbuf[i] = jnp.where(is0, filtered, advanced)
                for f in range(F):
                    snd[l, f] = zbuf[i, pl.ds(f, ROWS, stride=8), :]
            final_copy(c, g).start()
            for i in range(LV):
                l = LV * c + i
                zbuf[i] = jnp.where(is0, cur[l], prev[l])
                for f in range(F):
                    out[0, HALF * g + l, f] = zbuf[i, pl.ds(f, ROWS, stride=8), :]

        return carry

    lax.fori_loop(0, STEPS * CHUNKS, body, 0)

    for c in range(1, CHUNKS):
        tile_copy(c).wait_send()
    for c in range(CHUNKS):
        final_copy(c, g).wait_send()

    def drain(t, carry):
        for k in range(8):
            halo_copy(t, k).wait_send()
        return carry

    lax.fori_loop(0, STEPS * CHUNKS, drain, 0)
    for c in range(CHUNKS):
        final_copy(c, 1 - g).wait_recv()


def solution(mesh):
    nrow = mesh.shape["row"]
    ncol = mesh.shape["col"]

    def shards(fields, sea_mask, column_levels, w1, b1, w2, b2, w3, b3, w4, b4):
        vmem = pl.BlockSpec(memory_space=pltpu.VMEM)
        hbm = pl.BlockSpec(memory_space=pltpu.HBM)
        count = STEPS * CHUNKS
        operands = (
            fields,
            sea_mask,
            column_levels,
            w1,
            b1.reshape(1, -1),
            w2,
            b2.reshape(1, -1),
            w3,
            b3.reshape(1, -1),
            jnp.transpose(w4, (0, 1, 3, 2)),
            b4.reshape(1, -1),
        )
        dma = pltpu.SemaphoreType.DMA
        operands = tuple(pltpu.with_memory_space_constraint(x, pltpu.HBM) for x in operands)
        return pl.pallas_call(
            functools.partial(kernel, nrow, ncol),
            out_shape=jax.ShapeDtypeStruct(fields.shape, F32),
            in_specs=[hbm] * len(operands),
            out_specs=vmem,
            scratch_shapes=[
                pltpu.VMEM((HALF, F, ROWS, LANES), F32),
                *[pltpu.VMEM(x.shape, x.dtype) for x in operands[1:]],
                pltpu.VMEM((HALF, F, ROWS, LANES), F32),
                pltpu.VMEM((HALF, RF, LANES), F32),
                pltpu.VMEM((HALF, RF, LANES), F32),
                pltpu.VMEM((RF, LANES), F32),
                pltpu.VMEM((RF, LANES), F32),
                pltpu.VMEM((count, LV, 48, LANES), BF16),
                pltpu.VMEM((count, LV, 48, LANES), BF16),
                pltpu.VMEM((count, 3 * 8 * LV, LANES), BF16),
                pltpu.VMEM((count, 2, LV, 48, LANES), BF16),
                pltpu.VMEM((count, 2, 3 * 8 * LV, LANES), BF16),
                pltpu.VMEM((count, 4, 8 * LV, LANES), BF16),
                pltpu.VMEM((8 * TILES + 8, 256), BF16),
                pltpu.VMEM((2, 256, 256), BF16),
                pltpu.VMEM((1024, 256), BF16),
                pltpu.VMEM((1024, 256), BF16),
                pltpu.VMEM((512, 256), BF16),
                pltpu.VMEM((2, 256, 256), F32),
                pltpu.VMEM((3, 3, HID, LANES), F32),
                pltpu.VMEM((8, 256), F32),
                pltpu.VMEM((LV, 2, 192, 256), BF16),
                pltpu.VMEM((6, WIDE + 16, LANES), BF16),
                *[pltpu.VMEM((n, WIDE + 16, LANES), BF16) for n in (11, 11, 10, 10, 9, 9)],
                pltpu.VMEM((LV, 16 * TILES, LANES), F32),
                pltpu.VMEM((LV, RF, LANES), F32),
                pltpu.VMEM((2, RF, LANES), F32),
                pltpu.VMEM((HALF, F, ROWS, LANES), F32),
                dma((19 + 16 * count,)),
            ],
            compiler_params=pltpu.CompilerParams(
                collective_id=0,
                has_side_effects=True,
                vmem_limit_bytes=24 << 20,
            ),
        )(*operands)

    return jax.shard_map(
        shards,
        mesh=mesh,
        in_specs=(P("grp", None, None, "row", "col"), P("row", "col"), P("row", "col")) + (P(),) * 8,
        out_specs=P("grp", None, None, "row", "col"),
        check_vma=False,
    )
```
